32 devices in a mesh: lon: 8 (over z, x), lat: 4 (over y, core).
Axes of the slice: x: 2, y: 2, z: 4, core: 2. Of those that a mesh axis runs over, the one named last changes fastest.
Arguments:
- tokens: bfloat16 [96, 48, 512], P('lon', 'lat'), may hold values from -6 to 6
- norm_gain: float32 [512], replicated, may hold values from 0.5 to 1.5
- qkv_weight: bfloat16 [512, 1536], replicated, may hold values from -3 to 3
- bias_table: float32 [16, 529], replicated, may hold values from -8 to 260
- proj_weight: bfloat16 [512, 512], replicated, may hold values from -0.25 to 0.25
- out_grad: bfloat16 [96, 48, 512], P('lon', 'lat'), may hold values from -6 to 6
Outputs:
- token_grad: bfloat16 [96, 48, 512], P('lon', 'lat')
- qkv_grad: float32 [786432], P(('lon', 'lat'))
The draws below stay inside these ranges and needn't reach their ends.
All inputs are finite; a program needn't handle non-finite values.
Results may differ from the reference program's by a relative error of at most 0.0092.
Values may be sent and summed in bfloat16 or wider, within the bound.
No kernel may reach another device: no remote copies, remote signals or barrier semaphores. Data moves between devices by JAX's collectives and lax.ppermute only.
A program may use at most 128 MiB of HBM per device.

```python
import math
import jax
import jax.numpy as jnp
from jax import lax

D = 512
HEADS = 16
WIN = 12
SHIFT = 6
NLON = 96
NLAT = 48


def draw_qkv_weight(key, part):
    first = jax.random.fold_in(key, 0)
    matrix = jax.random.normal(first, (D, 3 * D), jnp.float32) * D ** (-0.5)
    return jnp.clip(matrix, -3.0, 3.0).astype(jnp.bfloat16)


def draw_bias_table(key, part):
    first = jax.random.fold_in(jax.random.fold_in(key, 7), 0)
    count = (2 * WIN - 1) * (2 * WIN - 1)
    rough = jax.random.normal(first, (HEADS, count), jnp.float32)
    table = jnp.clip(rough, -4.0, 4.0)
    return table


def block_levels(own_key, extent, cuts, smallest, largest):
    gain = 1.0
    for axis_at, parts in cuts:
        steps = jax.random.uniform(jax.random.fold_in(jax.random.fold_in(own_key, 6), axis_at), (parts,), jnp.float32, smallest / len(cuts), largest / len(cuts))
        gain = gain * jnp.repeat(jnp.exp(steps), extent[axis_at] // parts).reshape((-1,) + (1,) * (len(extent) - 1 - axis_at))
    return gain


def normal_values(rng, dims, spread, most, cuts=(), kind=jnp.bfloat16):
    level = block_levels(rng, dims, cuts, -0.22, 0.18) if cuts else 1.0
    drawn = jax.random.normal(rng, dims, jnp.float32) * spread * level
    return jnp.minimum(jnp.maximum(drawn, -most), most).astype(kind)


def setup_inputs(seed: int = 0) -> dict:
    key_list = jax.random.split(jax.random.key(seed), 7)
    tokens = normal_values(key_list[0], (NLON, NLAT, D), 1.0, 6.0, ((0, 8), (1, 4)))
    norm_gain = jnp.clip(1.0 + 0.1 * jax.random.normal(key_list[1], (D,), jnp.float32), 0.5, 1.5)
    qkv_weight = draw_qkv_weight(jax.random.fold_in(key_list[6], 71), 0)
    bias_table = draw_bias_table(jax.random.fold_in(key_list[6], 71), 0)
    proj_weight = normal_values(key_list[4], (D, D), D ** -0.5, 0.25)
    out_grad = normal_values(key_list[5], (NLON, NLAT, D), 1.0, 6.0, ((0, 8), (1, 4)))
    return {"tokens": tokens, "norm_gain": norm_gain, "qkv_weight": qkv_weight, "bias_table": bias_table, "proj_weight": proj_weight, "out_grad": out_grad}


def window_backward(shifted_tokens, shifted_grad, norm_gain, qkv_weight, bias_table, proj_weight, lat_start, lat_total):
    span_lon, span_lat, width = shifted_tokens.shape
    heads = bias_table.shape[0]
    head_size = width // heads
    edge = WIN // 2
    rows_lon = span_lon // WIN
    rows_lat = span_lat // WIN
    area = WIN * WIN
    factor = head_size ** (-0.5)
    inputs = shifted_tokens.astype(jnp.float32)
    centred = inputs - lax.optimization_barrier(jnp.mean(inputs, axis=-1, keepdims=True))
    inverse = lax.rsqrt(lax.optimization_barrier(jnp.mean(centred * centred, axis=-1, keepdims=True)) + 1e-05)
    unit = centred * inverse
    normed = (unit * norm_gain).astype(jnp.bfloat16).reshape(-1, width)
    projected = jnp.dot(normed, qkv_weight, preferred_element_type=jnp.float32).astype(jnp.bfloat16)
    blocks = projected.reshape(rows_lon, WIN, rows_lat, WIN, 3, heads, head_size)
    blocks = blocks.transpose(4, 0, 2, 5, 1, 3, 6).reshape(3, rows_lon, rows_lat, heads, area, head_size)
    query = blocks[0].astype(jnp.float32)
    keys = blocks[1].astype(jnp.float32)
    values = blocks[2].astype(jnp.float32)
    offsets = jnp.arange(2 * WIN - 1, dtype=jnp.int32)
    places = jnp.arange(WIN, dtype=jnp.int32)
    lookup = (places[:, None, None] - places[None, :, None] + WIN - 1 == offsets[None, None, :]).astype(jnp.float32)
    table = bias_table.reshape(heads, 2 * WIN - 1, 2 * WIN - 1)
    relative = jnp.einsum('hab,ija,klb->hikjl', table, lookup, lookup, precision=lax.Precision.HIGHEST).reshape(heads, area, area)
    position = lat_start + jnp.arange(span_lat, dtype=jnp.int32)
    group = (position >= lat_total - WIN).astype(jnp.int32) + (position >= lat_total - edge).astype(jnp.int32)
    group = jnp.broadcast_to(group.reshape(rows_lat, 1, WIN), (rows_lat, WIN, WIN)).reshape(rows_lat, area)
    allowed = (group[:, :, None] == group[:, None, :])[None, :, None]
    scores = jnp.einsum('nmhid,nmhjd->nmhij', query, keys) * factor + relative
    scores = jnp.where(allowed, scores, -1e+30)
    peak = lax.optimization_barrier(jnp.max(scores, axis=-1, keepdims=True))
    weights = jnp.exp(scores - peak)
    probs = weights / lax.optimization_barrier(jnp.sum(weights, axis=-1, keepdims=True))
    probs_low = probs.astype(jnp.bfloat16).astype(jnp.float32)
    upstream = jnp.dot(shifted_grad.reshape(-1, width), proj_weight.T, preferred_element_type=jnp.float32).astype(jnp.bfloat16)
    upstream = upstream.reshape(rows_lon, WIN, rows_lat, WIN, heads, head_size).transpose(0, 2, 4, 1, 3, 5)
    upstream = upstream.reshape(rows_lon, rows_lat, heads, area, head_size).astype(jnp.float32)
    grad_values = jnp.einsum('nmhij,nmhid->nmhjd', probs_low, upstream)
    grad_probs = jnp.einsum('nmhid,nmhjd->nmhij', upstream, values)
    centre = lax.optimization_barrier(jnp.sum(probs * grad_probs, axis=-1, keepdims=True))
    grad_scores = (probs * (grad_probs - centre) * factor).astype(jnp.bfloat16).astype(jnp.float32)
    grad_query = jnp.einsum('nmhij,nmhjd->nmhid', grad_scores, keys)
    grad_keys = jnp.einsum('nmhij,nmhid->nmhjd', grad_scores, query)
    stacked = jnp.stack([grad_query, grad_keys, grad_values]).astype(jnp.bfloat16)
    grad_qkv = stacked.reshape(3, rows_lon, rows_lat, heads, WIN, WIN, head_size)
    grad_qkv = grad_qkv.transpose(1, 4, 2, 5, 0, 3, 6).reshape(-1, 3 * width)
    grad_normed = jnp.dot(grad_qkv, qkv_weight.T, preferred_element_type=jnp.float32).reshape(span_lon, span_lat, width)
    scaled = grad_normed * norm_gain
    result = shifted_grad.astype(jnp.float32) + inverse * (scaled - lax.optimization_barrier(jnp.mean(scaled, axis=-1, keepdims=True)) - unit * lax.optimization_barrier(jnp.mean(scaled * unit, axis=-1, keepdims=True)))
    weight_grad = jnp.dot(grad_qkv.T, normed, preferred_element_type=jnp.float32)
    return (result.astype(jnp.bfloat16), weight_grad)

def reference(tokens, norm_gain, qkv_weight, bias_table, proj_weight, out_grad):
    shifted_tokens = jnp.roll(tokens, (-SHIFT, -SHIFT), axis=(0, 1))
    shifted_grad = jnp.roll(out_grad, (-SHIFT, -SHIFT), axis=(0, 1))
    bands = NLON // WIN
    token_rows = shifted_tokens.reshape(bands, WIN, NLAT, D)
    grad_rows = shifted_grad.reshape(bands, WIN, NLAT, D)

    def advance(total, pair):
        result, weight_grad = window_backward(pair[0], pair[1], norm_gain, qkv_weight, bias_table, proj_weight, 0, NLAT)
        return (total + weight_grad, result)
    total, results = lax.scan(advance, jnp.zeros((3 * D, D), jnp.float32), (token_rows, grad_rows))
    token_grad = jnp.roll(results.reshape(NLON, NLAT, D), (SHIFT, SHIFT), axis=(0, 1))
    qkv_grad = (total * (1.0 / math.sqrt(NLON * NLAT))).reshape(-1)
    return (token_grad, qkv_grad)
```

```python
import functools
import math

import jax
import jax.numpy as jnp
from jax import lax
from jax.experimental import pallas as pl
from jax.experimental.pallas import tpu as pltpu
from jax.sharding import PartitionSpec as P

WIN = 12
EDGE = WIN // 2
AREA = WIN * WIN
QUARTER = EDGE * EDGE
SPAN = 2 * WIN - 1
LANES = 128
F32 = jnp.float32
BF16 = jnp.bfloat16
AXES = ("lon", "lat")


def dot(a, b, ca, cb):
    return lax.dot_general(a, b, (((ca,), (cb,)), ((), ())), preferred_element_type=F32)


def bias_kernel(flag_ref, table_ref, low_ref, high_ref, pad_ref):
    heads, count = table_ref.shape
    width = pad_ref.shape[1]
    pad_ref[...] = jnp.zeros_like(pad_ref)
    pad_ref[:, :count] = table_ref[...]
    flat = pad_ref[...]
    shifts = WIN + EDGE
    moved = jnp.concatenate(
        [flat] + [pltpu.roll(flat, width - b, 1) for b in range(1, shifts)], axis=0
    )
    row = lax.broadcasted_iota(jnp.int32, (width, 2 * LANES), 0)
    col = lax.broadcasted_iota(jnp.int32, (width, 2 * LANES), 1)
    place = col + (SPAN - EDGE) * ((col * 10923) >> 16)
    pick = jnp.where((row == place) & (col < SPAN * EDGE), 1.0, 0.0).astype(BF16)
    first = moved.astype(BF16)
    rest = moved - first.astype(F32)
    second = rest.astype(BF16)
    third = (rest - second.astype(F32)).astype(BF16)
    packed = dot(first, pick, 1, 0) + (dot(second, pick, 1, 0) + dot(third, pick, 1, 0))
    half = WIN * EDGE
    lane = lax.broadcasted_iota(jnp.int32, (heads, LANES), 1)
    apart = jnp.where(flag_ref[0] > 0, -1e30, 0.0).astype(F32)
    for v in range(WIN):
        b = WIN - 1 - v
        side, inner = divmod(v, EDGE)
        near = packed[heads * b : heads * (b + 1)] + (apart if side == 1 else 0.0)
        far = packed[heads * (b + EDGE) : heads * (b + EDGE + 1)] + (apart if side == 0 else 0.0)
        for u in range(WIN):
            a = EDGE * (WIN - 1 - u)
            left = pltpu.roll(near, (2 * LANES - a) % (2 * LANES), 1) if a else near
            right = pltpu.roll(far, (half - a) % (2 * LANES), 1)
            start = heads * (side * half + u * EDGE + inner)
            low_ref[start : start + heads, :] = jnp.where(
                lane < half, left[:, :LANES], right[:, :LANES]
            )
            high_ref[start : start + heads, :] = right[:, LANES:]


def relative_bias(flag, table):
    heads = table.shape[0]
    shape = jax.ShapeDtypeStruct((AREA * heads, LANES), F32)
    width = -(-table.shape[1] // LANES) * LANES
    return pl.pallas_call(
        bias_kernel,
        out_shape=(shape, shape),
        in_specs=[
            pl.BlockSpec(memory_space=pltpu.SMEM),
            pl.BlockSpec(memory_space=pltpu.VMEM),
        ],
        out_specs=(pl.BlockSpec(memory_space=pltpu.VMEM),) * 2,
        scratch_shapes=[pltpu.VMEM((heads, width), F32)],
        cost_estimate=pl.CostEstimate(
            flops=2 * 3 * 18 * heads * width * 256, bytes_accessed=2 * AREA * heads * 512, transcendentals=0
        ),
        name="relative_bias",
    )(flag, table)


def window_kernel(
    blocks,
    order_ref,
    own_ref,
    lon_ref,
    lat_ref,
    diag_ref,
    gain_ref,
    weight_ref,
    proj_ref,
    low_ref,
    high_ref,
    own_out,
    lon_out,
    lat_out,
    diag_out,
    *rest,
):
    weight_outs = rest[:-5]
    token_ref, grad_ref, qkv_ref, turned_ref, placed_ref = rest[-5:]
    width = gain_ref.shape[1]
    heads = low_ref.shape[0] // AREA
    size = width // heads
    group = LANES // size
    factor = size ** (-0.5)
    for k, ref in enumerate((own_ref, lon_ref, lat_ref, diag_ref)):
        token_ref[QUARTER * k : QUARTER * (k + 1), :] = ref[0].astype(F32)
        grad_ref[QUARTER * k : QUARTER * (k + 1), :] = ref[1].astype(F32)
    inputs = token_ref[...]
    gain = gain_ref[...]
    centred = inputs - jnp.mean(inputs, axis=-1, keepdims=True)
    inverse = lax.rsqrt(jnp.mean(centred * centred, axis=-1, keepdims=True) + 1e-05)
    unit = centred * inverse
    normed = (unit * gain).astype(BF16)
    qkv_ref[...] = dot(normed, weight_ref[...], 1, 0).astype(BF16)
    upstream = dot(grad_ref[...].astype(BF16), proj_ref[...], 1, 1).astype(BF16)
    lane = lax.broadcasted_iota(jnp.int32, (AREA, LANES), 1)
    zero = jnp.zeros((AREA, LANES), BF16)
    for g in range(width // LANES):
        cols = slice(LANES * g, LANES * (g + 1))
        query = qkv_ref[:, LANES * g : LANES * (g + 1)]
        keys = qkv_ref[:, width + LANES * g : width + LANES * (g + 1)]
        values = qkv_ref[:, 2 * width + LANES * g : 2 * width + LANES * (g + 1)]
        up = upstream[:, cols]
        keys_turned = keys.T
        here = [(lane >= size * n) & (lane < size * (n + 1)) for n in range(group)]
        all_scores = dot(
            jnp.concatenate([jnp.where(m, keys, zero) for m in here], axis=0), query, 1, 1
        )
        all_grads = dot(
            jnp.concatenate([jnp.where(m, values, zero) for m in here], axis=0), up, 1, 1
        )
        grad_values = None
        for n in range(group):
            h = g * group + n
            rows = slice(AREA * n, AREA * (n + 1))
            bias = jnp.concatenate(
                [
                    low_ref[pl.ds(h, AREA, stride=heads), :],
                    high_ref[pl.ds(h, AREA, stride=heads), :],
                ],
                axis=1,
            )[:, :AREA]
            scores = all_scores[rows] * factor + bias
            peak = jnp.max(scores, axis=0, keepdims=True)
            weights = jnp.exp(scores - peak)
            probs = weights * (1.0 / jnp.sum(weights, axis=0, keepdims=True))
            grad_probs = all_grads[rows]
            centre = jnp.sum(probs * grad_probs, axis=0, keepdims=True)
            grad_scores = (probs * (grad_probs - centre) * factor).astype(BF16)
            part_values = dot(probs.astype(BF16), jnp.where(here[n], up, zero), 1, 0)
            part_keys = dot(grad_scores, jnp.where(here[n], query, zero), 1, 0)
            part_query = dot(keys_turned[size * n : size * (n + 1)], grad_scores, 1, 0)
            turned_ref[h * size : (h + 1) * size, :] = part_query.astype(BF16)
            if grad_values is None:
                grad_values, grad_keys = part_values, part_keys
            else:
                grad_values = grad_values + part_values
                grad_keys = grad_keys + part_keys
        grad_values = grad_values.astype(BF16)
        grad_keys = grad_keys.astype(BF16)
        qkv_ref[:, LANES * g : LANES * (g + 1)] = turned_ref[cols, :].T
        qkv_ref[:, width + LANES * g : width + LANES * (g + 1)] = grad_keys
        qkv_ref[:, 2 * width + LANES * g : 2 * width + LANES * (g + 1)] = grad_values
        turned_ref[width + LANES * g : width + LANES * (g + 1), :] = grad_keys.T
        turned_ref[2 * width + LANES * g : 2 * width + LANES * (g + 1), :] = grad_values.T
    grad_normed = dot(qkv_ref[...], weight_ref[...], 1, 1)
    scaled = grad_normed * gain
    result = grad_ref[...] + inverse * (
        scaled
        - jnp.mean(scaled, axis=-1, keepdims=True)
        - unit * jnp.mean(scaled * unit, axis=-1, keepdims=True)
    )
    token_ref[...] = result
    for k, ref in enumerate((own_out, lon_out, lat_out, diag_out)):
        ref[...] = token_ref[QUARTER * k : QUARTER * (k + 1), :].astype(BF16)
    if blocks is None:
        weight_outs[0][...] = dot(turned_ref[...], normed, 1, 0)
    else:
        rows = 3 * width // len(blocks)
        for slot, offset in enumerate(blocks):
            start = pl.multiple_of((order_ref[0] ^ offset) * rows, rows)
            placed_ref[slot * rows : (slot + 1) * rows, :] = turned_ref[pl.ds(start, rows), :]
        total = 3 * width // len(weight_outs)
        for k, ref in enumerate(weight_outs):
            ref[...] = dot(placed_ref[total * k : total * (k + 1), :], normed, 1, 0).astype(BF16)


def window_backward(order, quarters, gain, weight, proj, low, high, blocks):
    width = proj.shape[0]
    piece = jax.ShapeDtypeStruct((QUARTER, width), BF16)
    if blocks is None:
        weight_shapes = (jax.ShapeDtypeStruct((3 * width, width), F32),)
    else:
        weight_shapes = (jax.ShapeDtypeStruct((3 * width // 2, width), BF16),) * 2
    vmem = pl.BlockSpec(memory_space=pltpu.VMEM)
    return pl.pallas_call(
        functools.partial(window_kernel, blocks),
        out_shape=(piece,) * 4 + weight_shapes,
        in_specs=[pl.BlockSpec(memory_space=pltpu.SMEM)] + [vmem] * 9,
        out_specs=(vmem,) * (4 + len(weight_shapes)),
        scratch_shapes=[
            pltpu.VMEM((AREA, width), F32),
            pltpu.VMEM((AREA, width), F32),
            pltpu.VMEM((AREA, 3 * width), BF16),
            pltpu.VMEM((3 * width, AREA), BF16),
            pltpu.VMEM((3 * width, AREA), BF16),
        ],
        compiler_params=pltpu.CompilerParams(vmem_limit_bytes=32 << 20),
        cost_estimate=pl.CostEstimate(
            flops=2 * AREA * width * width * 10, bytes_accessed=6 << 20, transcendentals=16 * AREA * AREA
        ),
        name="window_backward",
    )(order, *quarters, gain, weight, proj, low, high)


def exchange(block, offset, total):
    return lax.ppermute(block, AXES, [(i, i ^ offset) for i in range(total)])


def gather_sum(slots, offsets, total):
    arrived = [exchange(slots[k + 1], offset, total) for k, offset in enumerate(offsets)]
    summed = slots[0].astype(F32)
    for piece in arrived:
        summed = summed + piece.astype(F32)
    return summed


def shards(tokens, norm_gain, qkv_weight, bias_table, proj_weight, out_grad):
    span_lon, span_lat, width = tokens.shape
    lons, lats = lax.axis_size("lon"), lax.axis_size("lat")
    total = lons * lats
    place = lax.axis_index("lon") * lats + lax.axis_index("lat")

    def route(step_lon, step_lat):
        return [
            (a * lats + b, (a + step_lon) % lons * lats + (b + step_lat) % lats)
            for a in range(lons)
            for b in range(lats)
        ]

    def quarter(at_lon, at_lat):
        return jnp.stack(
            [
                x[at_lon : at_lon + EDGE, at_lat : at_lat + EDGE].reshape(QUARTER, width)
                for x in (tokens, out_grad)
            ]
        )

    quarters = [
        quarter(EDGE, EDGE),
        lax.ppermute(quarter(0, EDGE), AXES, route(-1, 0)),
        lax.ppermute(quarter(EDGE, 0), AXES, route(0, -1)),
        lax.ppermute(quarter(0, 0), AXES, route(-1, -1)),
    ]
    flag = (lax.axis_index("lat") == lats - 1).astype(jnp.int32).reshape(1)
    low, high = relative_bias(flag, bias_table)
    rows = 3 * width // total
    staged = total % 32 == 0 and 3 * width % total == 0 and rows % 16 == 0
    if staged:
        far = total // 8
        blocks = tuple(
            core + 2 * plane + 8 * line
            for core in range(2)
            for plane in range(4)
            for line in range(far)
        )
    else:
        blocks = None
    own, to_lon, to_lat, to_diag, *weight_grads = window_backward(
        place.astype(jnp.int32).reshape(1),
        quarters,
        norm_gain.reshape(1, width),
        qkv_weight,
        proj_weight,
        low,
        high,
        blocks,
    )
    factor = 1.0 / math.sqrt(span_lon * lons * span_lat * lats)
    if staged:
        keep, send = weight_grads
        shape = (4, far, rows, width)
        pair = gather_sum([keep.reshape(shape), send.reshape(shape)], [1], total).astype(BF16)
        plane = gather_sum([pair[k] for k in range(4)], [2, 4, 6], total).astype(BF16)
        line = gather_sum([plane[k] for k in range(far)], [8 * k for k in range(1, far)], total)
        summed = line.reshape(-1)
    else:
        summed = lax.psum_scatter(
            weight_grads[0].reshape(-1), AXES, scatter_dimension=0, tiled=True
        )
    from_lon = lax.ppermute(to_lon, AXES, route(1, 0))
    from_lat = lax.ppermute(to_lat, AXES, route(0, 1))
    from_diag = lax.ppermute(to_diag, AXES, route(1, 1))
    cell = (EDGE, EDGE, width)
    upper = jnp.concatenate([from_diag.reshape(cell), from_lon.reshape(cell)], axis=1)
    lower = jnp.concatenate([from_lat.reshape(cell), own.reshape(cell)], axis=1)
    token_grad = jnp.concatenate([upper, lower], axis=0)
    return (token_grad, summed * factor)


def solution(mesh):
    placed = (P("lon", "lat", None), P(), P(), P(), P(), P("lon", "lat", None))
    return jax.shard_map(
        shards,
        mesh=mesh,
        in_specs=placed,
        out_specs=(P("lon", "lat", None), P(("lon", "lat"))),
        check_vma=False,
    )
```

```python
import functools
import math

import jax
import jax.numpy as jnp
from jax import lax
from jax.experimental import pallas as pl
from jax.experimental.pallas import tpu as pltpu
from jax.sharding import PartitionSpec as P

WIN = 12
EDGE = WIN // 2
AREA = WIN * WIN
QUARTER = EDGE * EDGE
SPAN = 2 * WIN - 1
LANES = 128
F32 = jnp.float32
BF16 = jnp.bfloat16
AXES = ("lon", "lat")


def dot(a, b, ca, cb):
    return lax.dot_general(a, b, (((ca,), (cb,)), ((), ())), preferred_element_type=F32)


def pack_kernel(
    tokens_hbm, grad_hbm, table_hbm, own_ref, lon_ref, lat_ref, diag_ref, table_ref, here_ref, stage_ref, sems
):
    copies = [
        pltpu.make_async_copy(tokens_hbm, here_ref.at[0], sems.at[0]),
        pltpu.make_async_copy(grad_hbm, here_ref.at[1], sems.at[1]),
        pltpu.make_async_copy(table_hbm, table_ref, sems.at[2]),
    ]
    for copy in copies:
        copy.start()
    for k in range(2):
        copies[k].wait()
        for u in range(WIN):
            line = here_ref[k, u].astype(F32)
            row = u % EDGE * EDGE
            early = u < EDGE
            stage_ref[k, 2 if early else 3, row : row + EDGE, :] = line[:EDGE]
            stage_ref[k, 0 if early else 1, row : row + EDGE, :] = line[EDGE:]
        for n, out in enumerate((own_ref, lon_ref, lat_ref, diag_ref)):
            out[k] = stage_ref[k, n].astype(BF16)
    copies[2].wait()


def pack(tokens, grad, table):
    width = tokens.shape[2]
    shape = jax.ShapeDtypeStruct((2, QUARTER, width), BF16)
    hbm = pl.BlockSpec(memory_space=pltpu.HBM)
    vmem = pl.BlockSpec(memory_space=pltpu.VMEM)
    return pl.pallas_call(
        pack_kernel,
        out_shape=(shape,) * 4 + (jax.ShapeDtypeStruct(table.shape, F32),),
        in_specs=[hbm] * 3,
        out_specs=(vmem,) * 5,
        scratch_shapes=[
            pltpu.VMEM((2,) + tokens.shape, BF16),
            pltpu.VMEM((2, 4, QUARTER, width), F32),
            pltpu.SemaphoreType.DMA((3,)),
        ],
        compiler_params=pltpu.CompilerParams(vmem_limit_bytes=8 << 20),
        cost_estimate=pl.CostEstimate(flops=0, bytes_accessed=1 << 20, transcendentals=0),
        name="pack",
    )(*(pltpu.with_memory_space_constraint(x, pltpu.HBM) for x in (tokens, grad, table)))


def bias_kernel(
    flag_ref, table_ref, weight_hbm, proj_hbm, low_ref, high_ref, weight_ref, proj_ref, pad_ref, sems
):
    copies = [
        pltpu.make_async_copy(weight_hbm, weight_ref, sems.at[0]),
        pltpu.make_async_copy(proj_hbm, proj_ref, sems.at[1]),
    ]
    for copy in copies:
        copy.start()
    heads, count = table_ref.shape
    width = pad_ref.shape[1]
    pad_ref[...] = jnp.zeros_like(pad_ref)
    pad_ref[:, :count] = table_ref[...]
    flat = pad_ref[...]
    shifts = WIN + EDGE
    moved = jnp.concatenate(
        [flat] + [pltpu.roll(flat, width - b, 1) for b in range(1, shifts)], axis=0
    )
    row = lax.broadcasted_iota(jnp.int32, (width, 2 * LANES), 0)
    col = lax.broadcasted_iota(jnp.int32, (width, 2 * LANES), 1)
    place = col + (SPAN - EDGE) * ((col * 10923) >> 16)
    pick = jnp.where((row == place) & (col < SPAN * EDGE), 1.0, 0.0).astype(BF16)
    first = moved.astype(BF16)
    rest = moved - first.astype(F32)
    second = rest.astype(BF16)
    third = (rest - second.astype(F32)).astype(BF16)
    packed = dot(first, pick, 1, 0) + (dot(second, pick, 1, 0) + dot(third, pick, 1, 0))
    half = WIN * EDGE
    lane = lax.broadcasted_iota(jnp.int32, (heads, LANES), 1)
    apart = jnp.where(flag_ref[0] > 0, -1e30, 0.0).astype(F32)
    for v in range(WIN):
        b = WIN - 1 - v
        side, inner = divmod(v, EDGE)
        near = packed[heads * b : heads * (b + 1)] + (apart if side == 1 else 0.0)
        far = packed[heads * (b + EDGE) : heads * (b + EDGE + 1)] + (apart if side == 0 else 0.0)
        for u in range(WIN):
            a = EDGE * (WIN - 1 - u)
            left = pltpu.roll(near, (2 * LANES - a) % (2 * LANES), 1) if a else near
            right = pltpu.roll(far, (half - a) % (2 * LANES), 1)
            start = heads * (side * half + u * EDGE + inner)
            low_ref[start : start + heads, :] = jnp.where(
                lane < half, left[:, :LANES], right[:, :LANES]
            )
            high_ref[start : start + heads, :] = right[:, LANES:]
    for copy in copies:
        copy.wait()


def relative_bias(flag, table, weight, proj):
    heads = table.shape[0]
    shape = jax.ShapeDtypeStruct((AREA * heads, LANES), F32)
    width = -(-table.shape[1] // LANES) * LANES
    hbm = pl.BlockSpec(memory_space=pltpu.HBM)
    vmem = pl.BlockSpec(memory_space=pltpu.VMEM)
    return pl.pallas_call(
        bias_kernel,
        out_shape=(
            shape,
            shape,
            jax.ShapeDtypeStruct(weight.shape, BF16),
            jax.ShapeDtypeStruct(proj.shape, BF16),
        ),
        in_specs=[pl.BlockSpec(memory_space=pltpu.SMEM), vmem, hbm, hbm],
        out_specs=(vmem,) * 4,
        scratch_shapes=[pltpu.VMEM((heads, width), F32), pltpu.SemaphoreType.DMA((2,))],
        compiler_params=pltpu.CompilerParams(vmem_limit_bytes=16 << 20),
        cost_estimate=pl.CostEstimate(
            flops=6 * 18 * heads * width * 256, bytes_accessed=6 << 20, transcendentals=0
        ),
        name="relative_bias",
    )(flag, table, *(pltpu.with_memory_space_constraint(x, pltpu.HBM) for x in (weight, proj)))


def window_kernel(
    blocks,
    order_ref,
    own_ref,
    lon_ref,
    lat_ref,
    diag_ref,
    gain_ref,
    weight_ref,
    proj_ref,
    low_ref,
    high_ref,
    own_out,
    lon_out,
    lat_out,
    diag_out,
    *rest,
):
    weight_outs = rest[:-5]
    token_ref, grad_ref, qkv_ref, turned_ref, placed_ref = rest[-5:]
    width = gain_ref.shape[1]
    heads = low_ref.shape[0] // AREA
    size = width // heads
    group = LANES // size
    factor = size ** (-0.5)
    for k, ref in enumerate((lon_ref, own_ref, diag_ref, lat_ref)):
        token_ref[QUARTER * k : QUARTER * (k + 1), :] = ref[0].astype(F32)
        grad_ref[QUARTER * k : QUARTER * (k + 1), :] = ref[1].astype(F32)
    inputs = token_ref[...]
    gain = gain_ref[...]
    centred = inputs - jnp.mean(inputs, axis=-1, keepdims=True)
    inverse = lax.rsqrt(jnp.mean(centred * centred, axis=-1, keepdims=True) + 1e-05)
    unit = centred * inverse
    normed = (unit * gain).astype(BF16)
    qkv_ref[...] = dot(normed, weight_ref[...], 1, 0).astype(BF16)
    upstream = dot(grad_ref[...].astype(BF16), proj_ref[...], 1, 1).astype(BF16)
    lane = lax.broadcasted_iota(jnp.int32, (AREA, LANES), 1)
    zero = jnp.zeros((AREA, LANES), BF16)
    for g in range(width // LANES):
        cols = slice(LANES * g, LANES * (g + 1))
        query = qkv_ref[:, LANES * g : LANES * (g + 1)]
        keys = qkv_ref[:, width + LANES * g : width + LANES * (g + 1)]
        values = qkv_ref[:, 2 * width + LANES * g : 2 * width + LANES * (g + 1)]
        up = upstream[:, cols]
        keys_turned = keys.T
        here = [(lane >= size * n) & (lane < size * (n + 1)) for n in range(group)]
        all_scores = dot(
            jnp.concatenate([jnp.where(m, keys, zero) for m in here], axis=0), query, 1, 1
        )
        all_grads = dot(
            jnp.concatenate([jnp.where(m, values, zero) for m in here], axis=0), up, 1, 1
        )
        grad_values = None
        for n in range(group):
            h = g * group + n
            rows = slice(AREA * n, AREA * (n + 1))
            bias = jnp.concatenate(
                [
                    low_ref[pl.ds(h, AREA, stride=heads), :],
                    high_ref[pl.ds(h, AREA, stride=heads), :],
                ],
                axis=1,
            )[:, :AREA]
            scores = all_scores[rows] * factor + bias
            peak = jnp.max(scores, axis=0, keepdims=True)
            weights = jnp.exp(scores - peak)
            probs = weights * (1.0 / jnp.sum(weights, axis=0, keepdims=True))
            grad_probs = all_grads[rows]
            centre = jnp.sum(probs * grad_probs, axis=0, keepdims=True)
            grad_scores = (probs * (grad_probs - centre) * factor).astype(BF16)
            part_values = dot(probs.astype(BF16), jnp.where(here[n], up, zero), 1, 0)
            part_keys = dot(grad_scores, jnp.where(here[n], query, zero), 1, 0)
            part_query = dot(keys_turned[size * n : size * (n + 1)], grad_scores, 1, 0)
            turned_ref[h * size : (h + 1) * size, :] = part_query.astype(BF16)
            if grad_values is None:
                grad_values, grad_keys = part_values, part_keys
            else:
                grad_values = grad_values + part_values
                grad_keys = grad_keys + part_keys
        grad_values = grad_values.astype(BF16)
        grad_keys = grad_keys.astype(BF16)
        qkv_ref[:, LANES * g : LANES * (g + 1)] = turned_ref[cols, :].T
        qkv_ref[:, width + LANES * g : width + LANES * (g + 1)] = grad_keys
        qkv_ref[:, 2 * width + LANES * g : 2 * width + LANES * (g + 1)] = grad_values
        turned_ref[width + LANES * g : width + LANES * (g + 1), :] = grad_keys.T
        turned_ref[2 * width + LANES * g : 2 * width + LANES * (g + 1), :] = grad_values.T
    grad_normed = dot(qkv_ref[...], weight_ref[...], 1, 1)
    scaled = grad_normed * gain
    result = grad_ref[...] + inverse * (
        scaled
        - jnp.mean(scaled, axis=-1, keepdims=True)
        - unit * jnp.mean(scaled * unit, axis=-1, keepdims=True)
    )
    token_ref[...] = result
    for k, ref in enumerate((lon_out, own_out, diag_out, lat_out)):
        ref[...] = token_ref[QUARTER * k : QUARTER * (k + 1), :].astype(BF16)
    if blocks is None:
        weight_outs[0][...] = dot(turned_ref[...], normed, 1, 0)
    else:
        rows = 3 * width // len(blocks)
        for slot, offset in enumerate(blocks):
            start = pl.multiple_of((order_ref[0] ^ offset) * rows, rows)
            placed_ref[slot * rows : (slot + 1) * rows, :] = turned_ref[pl.ds(start, rows), :]
        total = 3 * width // len(weight_outs)
        for k, ref in enumerate(weight_outs):
            ref[...] = dot(placed_ref[total * k : total * (k + 1), :], normed, 1, 0).astype(BF16)


def window_backward(order, quarters, gain, weight, proj, low, high, blocks):
    width = proj.shape[0]
    piece = jax.ShapeDtypeStruct((QUARTER, width), BF16)
    if blocks is None:
        weight_shapes = (jax.ShapeDtypeStruct((3 * width, width), F32),)
    else:
        weight_shapes = (jax.ShapeDtypeStruct((3 * width // 2, width), BF16),) * 2
    vmem = pl.BlockSpec(memory_space=pltpu.VMEM)
    return pl.pallas_call(
        functools.partial(window_kernel, blocks),
        out_shape=(piece,) * 4 + weight_shapes,
        in_specs=[pl.BlockSpec(memory_space=pltpu.SMEM)] + [vmem] * 9,
        out_specs=(vmem,) * (4 + len(weight_shapes)),
        scratch_shapes=[
            pltpu.VMEM((AREA, width), F32),
            pltpu.VMEM((AREA, width), F32),
            pltpu.VMEM((AREA, 3 * width), BF16),
            pltpu.VMEM((3 * width, AREA), BF16),
            pltpu.VMEM((3 * width, AREA), BF16),
        ],
        compiler_params=pltpu.CompilerParams(vmem_limit_bytes=32 << 20),
        cost_estimate=pl.CostEstimate(
            flops=2 * AREA * width * width * 10, bytes_accessed=6 << 20, transcendentals=16 * AREA * AREA
        ),
        name="window_backward",
    )(order, *quarters, gain, weight, proj, low, high)


def exchange(block, offset, total):
    return lax.ppermute(block, AXES, [(i, i ^ offset) for i in range(total)])


def send_slots(slots, offsets, total):
    return [exchange(slots[k + 1], offset, total) for k, offset in enumerate(offsets)]


def add_slots(own, arrived):
    summed = own.astype(F32)
    for piece in arrived:
        summed = summed + piece.astype(F32)
    return summed


def shards(tokens, norm_gain, qkv_weight, bias_table, proj_weight, out_grad):
    span_lon, span_lat, width = tokens.shape
    lons, lats = lax.axis_size("lon"), lax.axis_size("lat")
    total = lons * lats
    place = lax.axis_index("lon") * lats + lax.axis_index("lat")

    def route(step_lon, step_lat):
        return [
            (a * lats + b, (a + step_lon) % lons * lats + (b + step_lat) % lats)
            for a in range(lons)
            for b in range(lats)
        ]

    own, lon_start, lat_start, diag_start, table = pack(tokens, out_grad, bias_table)
    quarters = [
        own,
        lax.ppermute(lon_start, AXES, route(1, 0)),
        lax.ppermute(lat_start, AXES, route(0, -1)),
        lax.ppermute(diag_start, AXES, route(1, -1)),
    ]
    flag = (lax.axis_index("lat") == lats - 1).astype(jnp.int32).reshape(1)
    low, high, weight, proj = relative_bias(flag, table, qkv_weight, proj_weight)
    rows = 3 * width // total
    staged = total % 32 == 0 and 3 * width % total == 0 and rows % 16 == 0
    if staged:
        far = total // 8
        blocks = tuple(
            core + 2 * plane + 8 * line
            for core in range(2)
            for plane in range(4)
            for line in range(far)
        )
    else:
        blocks = None
    own, to_lon, to_lat, to_diag, *weight_grads = window_backward(
        place.astype(jnp.int32).reshape(1),
        quarters,
        norm_gain.reshape(1, width),
        weight,
        proj,
        low,
        high,
        blocks,
    )
    factor = 1.0 / math.sqrt(span_lon * lons * span_lat * lats)
    from_lon = lax.ppermute(to_lon, AXES, route(-1, 0))
    from_diag = lax.ppermute(to_diag, AXES, route(-1, 1))
    if staged:
        keep, send = weight_grads
        shape = (4, far, rows, width)
        pair = add_slots(keep.reshape(shape), [exchange(send.reshape(shape), 1, total)]).astype(BF16)
        plane = add_slots(pair[0], send_slots(pair, [2, 4, 6], total)).astype(BF16)
        plane, to_lat = lax.optimization_barrier((plane, to_lat))
        from_lat = lax.ppermute(to_lat, AXES, route(0, 1))
        arrived = send_slots(plane, [8 * k for k in range(1, far)], total)
        summed = add_slots(plane[0], arrived).reshape(-1)
    else:
        from_lat = lax.ppermute(to_lat, AXES, route(0, 1))
        summed = lax.psum_scatter(
            weight_grads[0].reshape(-1), AXES, scatter_dimension=0, tiled=True
        )
    cell = (EDGE, EDGE, width)
    upper = jnp.concatenate([from_lat.reshape(cell), own.reshape(cell)], axis=1)
    lower = jnp.concatenate([from_diag.reshape(cell), from_lon.reshape(cell)], axis=1)
    token_grad = jnp.concatenate([upper, lower], axis=0)
    return (token_grad, summed * factor)


def solution(mesh):
    placed = (P("lon", "lat", None), P(), P(), P(), P(), P("lon", "lat", None))
    return jax.shard_map(
        shards,
        mesh=mesh,
        in_specs=placed,
        out_specs=(P("lon", "lat", None), P(("lon", "lat"))),
        check_vma=False,
    )
```

```python
import functools
import math

import jax
import jax.numpy as jnp
from jax import lax
from jax.experimental import pallas as pl
from jax.experimental.pallas import tpu as pltpu
from jax.sharding import PartitionSpec as P

WIN = 12
EDGE = WIN // 2
AREA = WIN * WIN
QUARTER = EDGE * EDGE
SPAN = 2 * WIN - 1
LANES = 128
F32 = jnp.float32
BF16 = jnp.bfloat16
AXES = ("lon", "lat")
PLANE = (0, 2, 1, 3)


def line_order(far):
    return [0] + sorted(range(1, far), key=lambda k: (k != far // 2, k))


def dot(a, b, ca, cb):
    return lax.dot_general(a, b, (((ca,), (cb,)), ((), ())), preferred_element_type=F32)


def pack_kernel(
    tokens_hbm, grad_hbm, table_hbm, own_ref, lon_ref, lat_ref, diag_ref, table_ref, here_ref, stage_ref, sems
):
    copies = [
        pltpu.make_async_copy(tokens_hbm, here_ref.at[0], sems.at[0]),
        pltpu.make_async_copy(grad_hbm, here_ref.at[1], sems.at[1]),
        pltpu.make_async_copy(table_hbm, table_ref, sems.at[2]),
    ]
    for copy in copies:
        copy.start()
    for k in range(2):
        copies[k].wait()
        for u in range(WIN):
            line = here_ref[k, u].astype(F32)
            row = u % EDGE * EDGE
            early = u < EDGE
            row += k * QUARTER
            stage_ref[2 if early else 3, row : row + EDGE, :] = line[:EDGE]
            stage_ref[0 if early else 1, row : row + EDGE, :] = line[EDGE:]
    for n, out in enumerate((own_ref, lon_ref, lat_ref, diag_ref)):
        out[...] = stage_ref[n].astype(BF16)
    copies[2].wait()


def pack(tokens, grad, table):
    width = tokens.shape[2]
    shape = jax.ShapeDtypeStruct((2 * QUARTER, width), BF16)
    hbm = pl.BlockSpec(memory_space=pltpu.HBM)
    vmem = pl.BlockSpec(memory_space=pltpu.VMEM)
    return pl.pallas_call(
        pack_kernel,
        out_shape=(shape,) * 4 + (jax.ShapeDtypeStruct(table.shape, F32),),
        in_specs=[hbm] * 3,
        out_specs=(vmem,) * 5,
        scratch_shapes=[
            pltpu.VMEM((2,) + tokens.shape, BF16),
            pltpu.VMEM((4, 2 * QUARTER, width), F32),
            pltpu.SemaphoreType.DMA((3,)),
        ],
        compiler_params=pltpu.CompilerParams(vmem_limit_bytes=8 << 20),
        cost_estimate=pl.CostEstimate(flops=0, bytes_accessed=1 << 20, transcendentals=0),
        name="pack",
    )(*(pltpu.with_memory_space_constraint(x, pltpu.HBM) for x in (tokens, grad, table)))


def bias_kernel(
    flag_ref, table_ref, weight_hbm, proj_hbm, low_ref, high_ref, weight_ref, proj_ref, pad_ref, sems
):
    copies = []
    for source, target, chunks in ((weight_hbm, weight_ref, 6), (proj_hbm, proj_ref, 2)):
        step = source.shape[1] // chunks
        for k in range(chunks):
            part = pl.ds(k * step, step)
            copies.append(
                pltpu.make_async_copy(source.at[:, part], target.at[:, part], sems.at[len(copies)])
            )
    for copy in copies:
        copy.start()
    heads, count = table_ref.shape
    width = pad_ref.shape[1]
    pad_ref[...] = jnp.zeros_like(pad_ref)
    pad_ref[:, :count] = table_ref[...]
    flat = pad_ref[...]
    shifts = WIN + EDGE
    moved = jnp.concatenate(
        [flat] + [pltpu.roll(flat, width - b, 1) for b in range(1, shifts)], axis=0
    )
    row = lax.broadcasted_iota(jnp.int32, (width, 2 * LANES), 0)
    col = lax.broadcasted_iota(jnp.int32, (width, 2 * LANES), 1)
    place = col + (SPAN - EDGE) * ((col * 10923) >> 16)
    pick = jnp.where((row == place) & (col < SPAN * EDGE), 1.0, 0.0).astype(BF16)
    first = moved.astype(BF16)
    rest = moved - first.astype(F32)
    second = rest.astype(BF16)
    third = (rest - second.astype(F32)).astype(BF16)
    packed = dot(first, pick, 1, 0) + (dot(second, pick, 1, 0) + dot(third, pick, 1, 0))
    half = WIN * EDGE
    lane = lax.broadcasted_iota(jnp.int32, (heads, LANES), 1)
    apart = jnp.where(flag_ref[0] > 0, -1e30, 0.0).astype(F32)
    for v in range(WIN):
        b = WIN - 1 - v
        side, inner = divmod(v, EDGE)
        near = packed[heads * b : heads * (b + 1)] + (apart if side == 1 else 0.0)
        far = packed[heads * (b + EDGE) : heads * (b + EDGE + 1)] + (apart if side == 0 else 0.0)
        for u in range(WIN):
            a = EDGE * (WIN - 1 - u)
            left = pltpu.roll(near, (2 * LANES - a) % (2 * LANES), 1) if a else near
            right = pltpu.roll(far, (half - a) % (2 * LANES), 1)
            start = heads * (side * half + u * EDGE + inner)
            low_ref[start : start + heads, :] = jnp.where(
                lane < half, left[:, :LANES], right[:, :LANES]
            )
            high_ref[start : start + heads, :] = right[:, LANES:]
    for copy in copies:
        copy.wait()


def relative_bias(flag, table, weight, proj):
    heads = table.shape[0]
    shape = jax.ShapeDtypeStruct((AREA * heads, LANES), F32)
    width = -(-table.shape[1] // LANES) * LANES
    hbm = pl.BlockSpec(memory_space=pltpu.HBM)
    vmem = pl.BlockSpec(memory_space=pltpu.VMEM)
    return pl.pallas_call(
        bias_kernel,
        out_shape=(
            shape,
            shape,
            jax.ShapeDtypeStruct(weight.shape, BF16),
            jax.ShapeDtypeStruct(proj.shape, BF16),
        ),
        in_specs=[pl.BlockSpec(memory_space=pltpu.SMEM), vmem, hbm, hbm],
        out_specs=(vmem,) * 4,
        scratch_shapes=[pltpu.VMEM((heads, width), F32), pltpu.SemaphoreType.DMA((8,))],
        compiler_params=pltpu.CompilerParams(vmem_limit_bytes=16 << 20),
        cost_estimate=pl.CostEstimate(
            flops=6 * 18 * heads * width * 256, bytes_accessed=6 << 20, transcendentals=0
        ),
        name="relative_bias",
    )(flag, table, *(pltpu.with_memory_space_constraint(x, pltpu.HBM) for x in (weight, proj)))


def window_kernel(
    blocks,
    order_ref,
    own_ref,
    lon_ref,
    diag_ref,
    lat_ref,
    gain_ref,
    weight_ref,
    proj_ref,
    low_ref,
    high_ref,
    own_out,
    lon_out,
    lat_out,
    diag_out,
    *rest,
):
    weight_outs = rest[:-5]
    token_ref, grad_ref, qkv_ref, turned_ref, placed_ref = rest[-5:]
    width = gain_ref.shape[1]
    heads = low_ref.shape[0] // AREA
    size = width // heads
    group = LANES // size
    factor = size ** (-0.5)
    for k, ref in enumerate((lon_ref, own_ref, diag_ref, lat_ref)):
        both = ref[...].astype(F32)
        token_ref[QUARTER * k : QUARTER * (k + 1), :] = both[:QUARTER]
        grad_ref[QUARTER * k : QUARTER * (k + 1), :] = both[QUARTER:]
    inputs = token_ref[...]
    gain = gain_ref[...]
    centred = inputs - jnp.mean(inputs, axis=-1, keepdims=True)
    inverse = lax.rsqrt(jnp.mean(centred * centred, axis=-1, keepdims=True) + 1e-05)
    unit = centred * inverse
    normed = (unit * gain).astype(BF16)
    qkv_ref[...] = dot(normed, weight_ref[...], 1, 0).astype(BF16)
    upstream = dot(grad_ref[...].astype(BF16), proj_ref[...], 1, 1).astype(BF16)
    lane = lax.broadcasted_iota(jnp.int32, (AREA, LANES), 1)
    zero = jnp.zeros((AREA, LANES), BF16)
    for g in range(width // LANES):
        cols = slice(LANES * g, LANES * (g + 1))
        query = qkv_ref[:, LANES * g : LANES * (g + 1)]
        keys = qkv_ref[:, width + LANES * g : width + LANES * (g + 1)]
        values = qkv_ref[:, 2 * width + LANES * g : 2 * width + LANES * (g + 1)]
        up = upstream[:, cols]
        keys_turned = keys.T
        here = [(lane >= size * n) & (lane < size * (n + 1)) for n in range(group)]
        all_scores = dot(
            jnp.concatenate([jnp.where(m, keys, zero) for m in here], axis=0), query, 1, 1
        )
        all_grads = dot(
            jnp.concatenate([jnp.where(m, values, zero) for m in here], axis=0), up, 1, 1
        )
        low_probs, low_scores = [], []
        for n in range(group):
            h = g * group + n
            rows = slice(AREA * n, AREA * (n + 1))
            bias = jnp.concatenate(
                [
                    low_ref[pl.ds(h, AREA, stride=heads), :],
                    high_ref[pl.ds(h, AREA, stride=heads), :],
                ],
                axis=1,
            )[:, :AREA]
            scores = all_scores[rows] * factor + bias
            peak = jnp.max(scores, axis=0, keepdims=True)
            weights = jnp.exp(scores - peak)
            probs = weights * (1.0 / jnp.sum(weights, axis=0, keepdims=True))
            grad_probs = all_grads[rows]
            centre = jnp.sum(probs * grad_probs, axis=0, keepdims=True)
            grad_scores = (probs * (grad_probs - centre) * factor).astype(BF16)
            low_probs.append(probs.astype(BF16))
            low_scores.append(grad_scores)
            part_query = dot(keys_turned[size * n : size * (n + 1)], grad_scores, 1, 0)
            turned_ref[h * size : (h + 1) * size, :] = part_query.astype(BF16)
        all_values = dot(jnp.concatenate(low_probs, axis=0), up, 1, 0)
        all_keys = dot(jnp.concatenate(low_scores, axis=0), query, 1, 0)
        grad_values, grad_keys = all_values[:AREA], all_keys[:AREA]
        for n in range(1, group):
            rows = slice(AREA * n, AREA * (n + 1))
            grad_values = jnp.where(here[n], all_values[rows], grad_values)
            grad_keys = jnp.where(here[n], all_keys[rows], grad_keys)
        grad_values = grad_values.astype(BF16)
        grad_keys = grad_keys.astype(BF16)
        qkv_ref[:, LANES * g : LANES * (g + 1)] = turned_ref[cols, :].T
        qkv_ref[:, width + LANES * g : width + LANES * (g + 1)] = grad_keys
        qkv_ref[:, 2 * width + LANES * g : 2 * width + LANES * (g + 1)] = grad_values
        turned_ref[width + LANES * g : width + LANES * (g + 1), :] = grad_keys.T
        turned_ref[2 * width + LANES * g : 2 * width + LANES * (g + 1), :] = grad_values.T
    grad_normed = dot(qkv_ref[...], weight_ref[...], 1, 1)
    scaled = grad_normed * gain
    result = grad_ref[...] + inverse * (
        scaled
        - jnp.mean(scaled, axis=-1, keepdims=True)
        - unit * jnp.mean(scaled * unit, axis=-1, keepdims=True)
    )
    token_ref[...] = result
    for k, ref in enumerate((lon_out, own_out, diag_out, lat_out)):
        ref[...] = token_ref[QUARTER * k : QUARTER * (k + 1), :].astype(BF16)
    if blocks is None:
        weight_outs[0][...] = dot(turned_ref[...], normed, 1, 0)
    else:
        rows = 3 * width // len(blocks)
        place = order_ref[0]
        odd = place % 2 == 1
        for slot, (even_offset, odd_offset) in enumerate(blocks):
            offset = jnp.where(odd, odd_offset, even_offset)
            start = pl.multiple_of((place ^ offset) * rows, rows)
            placed_ref[slot * rows : (slot + 1) * rows, :] = turned_ref[pl.ds(start, rows), :]
        total = 3 * width // len(weight_outs)
        for k, ref in enumerate(weight_outs):
            ref[...] = dot(placed_ref[total * k : total * (k + 1), :], normed, 1, 0).astype(BF16)


def window_backward(order, quarters, gain, weight, proj, low, high, blocks):
    width = proj.shape[0]
    piece = jax.ShapeDtypeStruct((QUARTER, width), BF16)
    if blocks is None:
        weight_shapes = (jax.ShapeDtypeStruct((3 * width, width), F32),)
    else:
        weight_shapes = (jax.ShapeDtypeStruct((3 * width // 2, width), BF16),) * 2
    vmem = pl.BlockSpec(memory_space=pltpu.VMEM)
    return pl.pallas_call(
        functools.partial(window_kernel, blocks),
        out_shape=(piece,) * 4 + weight_shapes,
        in_specs=[pl.BlockSpec(memory_space=pltpu.SMEM)] + [vmem] * 9,
        out_specs=(vmem,) * (4 + len(weight_shapes)),
        scratch_shapes=[
            pltpu.VMEM((AREA, width), F32),
            pltpu.VMEM((AREA, width), F32),
            pltpu.VMEM((AREA, 3 * width), BF16),
            pltpu.VMEM((3 * width, AREA), BF16),
            pltpu.VMEM((3 * width, AREA), BF16),
        ],
        compiler_params=pltpu.CompilerParams(vmem_limit_bytes=32 << 20),
        cost_estimate=pl.CostEstimate(
            flops=2 * AREA * width * width * 10, bytes_accessed=6 << 20, transcendentals=16 * AREA * AREA
        ),
        name="window_backward",
    )(order, *quarters, gain, weight, proj, low, high)


def exchange(block, even, odd, total):
    pairs = [(i, i ^ (odd if i % 2 else even)) for i in range(total)]
    return lax.ppermute(block, AXES, pairs)


def send_slots(slots, offsets, total):
    return [exchange(slots[k + 1], *offset, total) for k, offset in enumerate(offsets)]


def add_slots(own, arrived):
    summed = own.astype(F32)
    for piece in arrived:
        summed = summed + piece.astype(F32)
    return summed


def shards(tokens, norm_gain, qkv_weight, bias_table, proj_weight, out_grad):
    span_lon, span_lat, width = tokens.shape
    lons, lats = lax.axis_size("lon"), lax.axis_size("lat")
    total = lons * lats
    place = lax.axis_index("lon") * lats + lax.axis_index("lat")

    def route(step_lon, step_lat):
        return [
            (a * lats + b, (a + step_lon) % lons * lats + (b + step_lat) % lats)
            for a in range(lons)
            for b in range(lats)
        ]

    own, lon_start, lat_start, diag_start, table = pack(tokens, out_grad, bias_table)
    at_lon = lax.ppermute(lon_start, AXES, route(1, 0))
    at_diag = lax.ppermute(diag_start, AXES, route(1, -1))
    at_lat = lax.ppermute(lat_start, AXES, route(0, -1))
    quarters = [own, at_lon, at_diag, at_lat]
    flag = (lax.axis_index("lat") == lats - 1).astype(jnp.int32).reshape(1)
    low, high, weight, proj = relative_bias(flag, table, qkv_weight, proj_weight)
    rows = 3 * width // total
    staged = total % 32 == 0 and 3 * width % total == 0 and rows % 16 == 0
    if staged:
        far = total // 8
        blocks = tuple(
            (core + 2 * (k if core else PLANE[k]) + 8 * line, core + 2 * (PLANE[k] if core else k) + 8 * line)
            for core in range(2)
            for k in range(4)
            for line in line_order(far)
        )
    else:
        blocks = None
    own, to_lon, to_lat, to_diag, *weight_grads = window_backward(
        place.astype(jnp.int32).reshape(1),
        quarters,
        norm_gain.reshape(1, width),
        weight,
        proj,
        low,
        high,
        blocks,
    )
    factor = 1.0 / math.sqrt(span_lon * lons * span_lat * lats)
    from_lon = lax.ppermute(to_lon, AXES, route(-1, 0))
    from_diag = lax.ppermute(to_diag, AXES, route(-1, 1))
    if staged:
        keep, send = weight_grads
        shape = (4, far, rows, width)
        pair = add_slots(keep.reshape(shape), [exchange(send.reshape(shape), 1, 1, total)]).astype(BF16)
        plane = add_slots(pair[0], send_slots(pair, [(2 * PLANE[k], 2 * k) for k in range(1, 4)], total)).astype(BF16)
        from_lat = lax.ppermute(to_lat, AXES, route(0, 1))
        arrived = send_slots(plane, [(8 * k, 8 * k) for k in line_order(far)[1:]], total)
        summed = add_slots(plane[0], arrived).reshape(-1)
    else:
        from_lat = lax.ppermute(to_lat, AXES, route(0, 1))
        summed = lax.psum_scatter(
            weight_grads[0].reshape(-1), AXES, scatter_dimension=0, tiled=True
        )
    cell = (EDGE, EDGE, width)
    upper = jnp.concatenate([from_lat.reshape(cell), own.reshape(cell)], axis=1)
    lower = jnp.concatenate([from_diag.reshape(cell), from_lon.reshape(cell)], axis=1)
    token_grad = jnp.concatenate([upper, lower], axis=0)
    return (token_grad, summed * factor)


def solution(mesh):
    placed = (P("lon", "lat", None), P(), P(), P(), P(), P("lon", "lat", None))
    return jax.shard_map(
        shards,
        mesh=mesh,
        in_specs=placed,
        out_specs=(P("lon", "lat", None), P(("lon", "lat"))),
        check_vma=False,
    )
```

```python
import functools
import math

import jax
import jax.numpy as jnp
from jax import lax
from jax.experimental import pallas as pl
from jax.experimental.pallas import tpu as pltpu
from jax.sharding import PartitionSpec as P

WIN = 12
EDGE = WIN // 2
AREA = WIN * WIN
QUARTER = EDGE * EDGE
SPAN = 2 * WIN - 1
LANES = 128
F32 = jnp.float32
BF16 = jnp.bfloat16
AXES = ("lon", "lat")
PLANE = (0, 2, 1, 3)


def line_order(far):
    return [0] + sorted(range(1, far), key=lambda k: (k != far // 2, k))


def dot(a, b, ca, cb):
    return lax.dot_general(a, b, (((ca,), (cb,)), ((), ())), preferred_element_type=F32)


def pack_kernel(
    tokens_hbm, grad_hbm, table_hbm, own_ref, lon_ref, lat_ref, diag_ref, table_ref, here_ref, stage_ref, sems
):
    copies = [
        pltpu.make_async_copy(tokens_hbm, here_ref.at[0], sems.at[0]),
        pltpu.make_async_copy(grad_hbm, here_ref.at[1], sems.at[1]),
        pltpu.make_async_copy(table_hbm, table_ref, sems.at[2]),
    ]
    for copy in copies:
        copy.start()
    for k in range(2):
        copies[k].wait()
        for u in range(WIN):
            line = here_ref[k, u].astype(F32)
            row = u % EDGE * EDGE
            early = u < EDGE
            row += k * QUARTER
            stage_ref[2 if early else 3, row : row + EDGE, :] = line[:EDGE]
            stage_ref[0 if early else 1, row : row + EDGE, :] = line[EDGE:]
    for n, out in enumerate((own_ref, lon_ref, lat_ref, diag_ref)):
        out[...] = stage_ref[n].astype(BF16)
    copies[2].wait()


def pack(tokens, grad, table):
    width = tokens.shape[2]
    shape = jax.ShapeDtypeStruct((2 * QUARTER, width), BF16)
    hbm = pl.BlockSpec(memory_space=pltpu.HBM)
    vmem = pl.BlockSpec(memory_space=pltpu.VMEM)
    return pl.pallas_call(
        pack_kernel,
        out_shape=(shape,) * 4 + (jax.ShapeDtypeStruct(table.shape, F32),),
        in_specs=[hbm] * 3,
        out_specs=(vmem,) * 5,
        scratch_shapes=[
            pltpu.VMEM((2,) + tokens.shape, BF16),
            pltpu.VMEM((4, 2 * QUARTER, width), F32),
            pltpu.SemaphoreType.DMA((3,)),
        ],
        compiler_params=pltpu.CompilerParams(vmem_limit_bytes=8 << 20),
        cost_estimate=pl.CostEstimate(flops=0, bytes_accessed=1 << 20, transcendentals=0),
        name="pack",
    )(*(pltpu.with_memory_space_constraint(x, pltpu.HBM) for x in (tokens, grad, table)))


def bias_kernel(
    flag_ref, table_ref, weight_hbm, proj_hbm, low_ref, high_ref, weight_ref, proj_ref, pad_ref, sems
):
    copies = []
    for source, target, chunks in ((weight_hbm, weight_ref, 6), (proj_hbm, proj_ref, 2)):
        step = source.shape[1] // chunks
        for k in range(chunks):
            part = pl.ds(k * step, step)
            copies.append(
                pltpu.make_async_copy(source.at[:, part], target.at[:, part], sems.at[len(copies)])
            )
    for copy in copies:
        copy.start()
    heads, count = table_ref.shape
    width = pad_ref.shape[1]
    pad_ref[...] = jnp.zeros_like(pad_ref)
    pad_ref[:, :count] = table_ref[...]
    flat = pad_ref[...]
    shifts = WIN + EDGE
    moved = jnp.concatenate(
        [flat] + [pltpu.roll(flat, width - b, 1) for b in range(1, shifts)], axis=0
    )
    row = lax.broadcasted_iota(jnp.int32, (width, 2 * LANES), 0)
    col = lax.broadcasted_iota(jnp.int32, (width, 2 * LANES), 1)
    place = col + (SPAN - EDGE) * ((col * 10923) >> 16)
    pick = jnp.where((row == place) & (col < SPAN * EDGE), 1.0, 0.0).astype(BF16)
    first = moved.astype(BF16)
    rest = moved - first.astype(F32)
    second = rest.astype(BF16)
    third = (rest - second.astype(F32)).astype(BF16)
    packed = dot(first, pick, 1, 0) + (dot(second, pick, 1, 0) + dot(third, pick, 1, 0))
    half = WIN * EDGE
    lane = lax.broadcasted_iota(jnp.int32, (heads, LANES), 1)
    apart = jnp.where(flag_ref[0] > 0, -1e30, 0.0).astype(F32)
    for v in range(WIN):
        b = WIN - 1 - v
        side, inner = divmod(v, EDGE)
        near = packed[heads * b : heads * (b + 1)] + (apart if side == 1 else 0.0)
        far = packed[heads * (b + EDGE) : heads * (b + EDGE + 1)] + (apart if side == 0 else 0.0)
        for u in range(WIN):
            a = EDGE * (WIN - 1 - u)
            left = pltpu.roll(near, (2 * LANES - a) % (2 * LANES), 1) if a else near
            right = pltpu.roll(far, (half - a) % (2 * LANES), 1)
            start = heads * (side * half + u * EDGE + inner)
            low_ref[start : start + heads, :] = jnp.where(
                lane < half, left[:, :LANES], right[:, :LANES]
            )
            high_ref[start : start + heads, :] = right[:, LANES:]
    for copy in copies:
        copy.wait()


def relative_bias(flag, table, weight, proj):
    heads = table.shape[0]
    shape = jax.ShapeDtypeStruct((AREA * heads, LANES), F32)
    width = -(-table.shape[1] // LANES) * LANES
    hbm = pl.BlockSpec(memory_space=pltpu.HBM)
    vmem = pl.BlockSpec(memory_space=pltpu.VMEM)
    return pl.pallas_call(
        bias_kernel,
        out_shape=(
            shape,
            shape,
            jax.ShapeDtypeStruct(weight.shape, BF16),
            jax.ShapeDtypeStruct(proj.shape, BF16),
        ),
        in_specs=[pl.BlockSpec(memory_space=pltpu.SMEM), vmem, hbm, hbm],
        out_specs=(vmem,) * 4,
        scratch_shapes=[pltpu.VMEM((heads, width), F32), pltpu.SemaphoreType.DMA((8,))],
        compiler_params=pltpu.CompilerParams(vmem_limit_bytes=16 << 20),
        cost_estimate=pl.CostEstimate(
            flops=6 * 18 * heads * width * 256, bytes_accessed=6 << 20, transcendentals=0
        ),
        name="relative_bias",
    )(flag, table, *(pltpu.with_memory_space_constraint(x, pltpu.HBM) for x in (weight, proj)))


def window_kernel(
    blocks,
    order_ref,
    own_ref,
    lon_ref,
    diag_ref,
    lat_ref,
    gain_ref,
    weight_ref,
    proj_ref,
    low_ref,
    high_ref,
    qkv_ref,
    unit_ref,
    inverse_ref,
    grad_ref,
    *rest,
):
    weight_outs = rest[:-3]
    token_ref, turned_ref, placed_ref = rest[-3:]
    width = gain_ref.shape[1]
    heads = low_ref.shape[0] // AREA
    size = width // heads
    group = LANES // size
    factor = size ** (-0.5)
    for k, ref in enumerate((lon_ref, own_ref, diag_ref, lat_ref)):
        both = ref[...].astype(F32)
        token_ref[QUARTER * k : QUARTER * (k + 1), :] = both[:QUARTER]
        grad_ref[QUARTER * k : QUARTER * (k + 1), :] = both[QUARTER:]
    inputs = token_ref[...]
    gain = gain_ref[...]
    centred = inputs - jnp.mean(inputs, axis=-1, keepdims=True)
    inverse = lax.rsqrt(jnp.mean(centred * centred, axis=-1, keepdims=True) + 1e-05)
    unit = centred * inverse
    unit_ref[...] = unit
    inverse_ref[...] = jnp.broadcast_to(inverse, inverse_ref.shape)
    normed = (unit * gain).astype(BF16)
    qkv_ref[...] = dot(normed, weight_ref[...], 1, 0).astype(BF16)
    upstream = dot(grad_ref[...].astype(BF16), proj_ref[...], 1, 1).astype(BF16)
    lane = lax.broadcasted_iota(jnp.int32, (AREA, LANES), 1)
    zero = jnp.zeros((AREA, LANES), BF16)
    for g in range(width // LANES):
        cols = slice(LANES * g, LANES * (g + 1))
        query = qkv_ref[:, LANES * g : LANES * (g + 1)]
        keys = qkv_ref[:, width + LANES * g : width + LANES * (g + 1)]
        values = qkv_ref[:, 2 * width + LANES * g : 2 * width + LANES * (g + 1)]
        up = upstream[:, cols]
        keys_turned = keys.T
        here = [(lane >= size * n) & (lane < size * (n + 1)) for n in range(group)]
        all_scores = dot(
            jnp.concatenate([jnp.where(m, keys, zero) for m in here], axis=0), query, 1, 1
        )
        all_grads = dot(
            jnp.concatenate([jnp.where(m, values, zero) for m in here], axis=0), up, 1, 1
        )
        low_probs, low_scores = [], []
        for n in range(group):
            h = g * group + n
            rows = slice(AREA * n, AREA * (n + 1))
            bias = jnp.concatenate(
                [
                    low_ref[pl.ds(h, AREA, stride=heads), :],
                    high_ref[pl.ds(h, AREA, stride=heads), :],
                ],
                axis=1,
            )[:, :AREA]
            scores = all_scores[rows] * factor + bias
            peak = jnp.max(scores, axis=0, keepdims=True)
            weights = jnp.exp(scores - peak)
            probs = weights * (1.0 / jnp.sum(weights, axis=0, keepdims=True))
            grad_probs = all_grads[rows]
            centre = jnp.sum(probs * grad_probs, axis=0, keepdims=True)
            grad_scores = (probs * (grad_probs - centre) * factor).astype(BF16)
            low_probs.append(probs.astype(BF16))
            low_scores.append(grad_scores)
            part_query = dot(keys_turned[size * n : size * (n + 1)], grad_scores, 1, 0)
            turned_ref[h * size : (h + 1) * size, :] = part_query.astype(BF16)
        all_values = dot(jnp.concatenate(low_probs, axis=0), up, 1, 0)
        all_keys = dot(jnp.concatenate(low_scores, axis=0), query, 1, 0)
        grad_values, grad_keys = all_values[:AREA], all_keys[:AREA]
        for n in range(1, group):
            rows = slice(AREA * n, AREA * (n + 1))
            grad_values = jnp.where(here[n], all_values[rows], grad_values)
            grad_keys = jnp.where(here[n], all_keys[rows], grad_keys)
        grad_values = grad_values.astype(BF16)
        grad_keys = grad_keys.astype(BF16)
        qkv_ref[:, LANES * g : LANES * (g + 1)] = turned_ref[cols, :].T
        qkv_ref[:, width + LANES * g : width + LANES * (g + 1)] = grad_keys
        qkv_ref[:, 2 * width + LANES * g : 2 * width + LANES * (g + 1)] = grad_values
        turned_ref[width + LANES * g : width + LANES * (g + 1), :] = grad_keys.T
        turned_ref[2 * width + LANES * g : 2 * width + LANES * (g + 1), :] = grad_values.T
    if blocks is None:
        weight_outs[0][...] = dot(turned_ref[...], normed, 1, 0)
    else:
        rows = 3 * width // len(blocks)
        place = order_ref[0]
        odd = place % 2 == 1
        for slot, (even_offset, odd_offset) in enumerate(blocks):
            offset = jnp.where(odd, odd_offset, even_offset)
            start = pl.multiple_of((place ^ offset) * rows, rows)
            placed_ref[slot * rows : (slot + 1) * rows, :] = turned_ref[pl.ds(start, rows), :]
        total = 3 * width // len(weight_outs)
        for k, ref in enumerate(weight_outs):
            ref[...] = dot(placed_ref[total * k : total * (k + 1), :], normed, 1, 0).astype(BF16)


def window_backward(order, quarters, gain, weight, proj, low, high, blocks):
    width = proj.shape[0]
    if blocks is None:
        weight_shapes = (jax.ShapeDtypeStruct((3 * width, width), F32),)
    else:
        weight_shapes = (jax.ShapeDtypeStruct((3 * width // 2, width), BF16),) * 2
    vmem = pl.BlockSpec(memory_space=pltpu.VMEM)
    return pl.pallas_call(
        functools.partial(window_kernel, blocks),
        out_shape=(
            jax.ShapeDtypeStruct((AREA, 3 * width), BF16),
            jax.ShapeDtypeStruct((AREA, width), F32),
            jax.ShapeDtypeStruct((AREA, LANES), F32),
            jax.ShapeDtypeStruct((AREA, width), F32),
        )
        + weight_shapes,
        in_specs=[pl.BlockSpec(memory_space=pltpu.SMEM)] + [vmem] * 9,
        out_specs=(vmem,) * (4 + len(weight_shapes)),
        scratch_shapes=[
            pltpu.VMEM((AREA, width), F32),
            pltpu.VMEM((3 * width, AREA), BF16),
            pltpu.VMEM((3 * width, AREA), BF16),
        ],
        compiler_params=pltpu.CompilerParams(vmem_limit_bytes=32 << 20),
        cost_estimate=pl.CostEstimate(
            flops=2 * AREA * width * width * 7, bytes_accessed=6 << 20, transcendentals=16 * AREA * AREA
        ),
        name="window_backward",
    )(order, *quarters, gain, weight, proj, low, high)


def norm_kernel(
    qkv_ref, weight_ref, gain_ref, unit_ref, inverse_ref, grad_ref, own_out, lon_out, side_out, token_ref
):
    unit = unit_ref[...]
    scaled = dot(qkv_ref[...], weight_ref[...], 1, 1) * gain_ref[...]
    result = grad_ref[...] + inverse_ref[:, :1] * (
        scaled
        - jnp.mean(scaled, axis=-1, keepdims=True)
        - unit * jnp.mean(scaled * unit, axis=-1, keepdims=True)
    )
    token_ref[...] = result
    for k, ref in enumerate((lon_out, own_out, side_out.at[1], side_out.at[0])):
        ref[...] = token_ref[QUARTER * k : QUARTER * (k + 1), :].astype(BF16)


def norm_backward(qkv, weight, gain, unit, inverse, grad):
    width = unit.shape[1]
    piece = jax.ShapeDtypeStruct((QUARTER, width), BF16)
    vmem = pl.BlockSpec(memory_space=pltpu.VMEM)
    return pl.pallas_call(
        norm_kernel,
        out_shape=(piece, piece, jax.ShapeDtypeStruct((2, QUARTER, width), BF16)),
        in_specs=[vmem] * 6,
        out_specs=(vmem,) * 3,
        scratch_shapes=[pltpu.VMEM((AREA, width), F32)],
        compiler_params=pltpu.CompilerParams(vmem_limit_bytes=16 << 20),
        cost_estimate=pl.CostEstimate(
            flops=6 * AREA * width * width, bytes_accessed=3 << 20, transcendentals=0
        ),
        name="norm_backward",
    )(qkv, weight, gain, unit, inverse, grad)


def unpack_kernel(lon_ref, side_ref, own_ref, out_ref, line_ref):
    for u in range(WIN):
        left, right = (side_ref[0], own_ref[...]) if u < EDGE else (lon_ref[1], lon_ref[0])
        rows = slice(u % EDGE * EDGE, u % EDGE * EDGE + EDGE)
        line_ref[u, :EDGE, :] = left.astype(F32)[rows]
        line_ref[u, EDGE:, :] = right.astype(F32)[rows]
    out_ref[...] = line_ref[...].astype(BF16)


def unpack(lon, side, own):
    width = own.shape[1]
    vmem = pl.BlockSpec(memory_space=pltpu.VMEM)
    return pl.pallas_call(
        unpack_kernel,
        out_shape=jax.ShapeDtypeStruct((WIN, WIN, width), BF16),
        in_specs=[vmem] * 3,
        out_specs=vmem,
        scratch_shapes=[pltpu.VMEM((WIN, WIN, width), F32)],
        compiler_params=pltpu.CompilerParams(vmem_limit_bytes=8 << 20),
        cost_estimate=pl.CostEstimate(flops=0, bytes_accessed=1 << 19, transcendentals=0),
        name="unpack",
    )(lon, side, own)


def exchange(block, even, odd, total):
    pairs = [(i, i ^ (odd if i % 2 else even)) for i in range(total)]
    return lax.ppermute(block, AXES, pairs)


def send_slots(slots, offsets, total):
    return [exchange(slots[k + 1], *offset, total) for k, offset in enumerate(offsets)]


def add_slots(own, arrived):
    summed = own.astype(F32)
    for piece in arrived:
        summed = summed + piece.astype(F32)
    return summed


def shards(tokens, norm_gain, qkv_weight, bias_table, proj_weight, out_grad):
    span_lon, span_lat, width = tokens.shape
    lons, lats = lax.axis_size("lon"), lax.axis_size("lat")
    total = lons * lats
    place = lax.axis_index("lon") * lats + lax.axis_index("lat")

    def route(step_lon, step_lat):
        return [
            (a * lats + b, (a + step_lon) % lons * lats + (b + step_lat) % lats)
            for a in range(lons)
            for b in range(lats)
        ]

    own, lon_start, lat_start, diag_start, table = pack(tokens, out_grad, bias_table)
    at_lon = lax.ppermute(lon_start, AXES, route(1, 0))
    at_diag = lax.ppermute(diag_start, AXES, route(1, -1))
    at_lat = lax.ppermute(lat_start, AXES, route(0, -1))
    quarters = [own, at_lon, at_diag, at_lat]
    flag = (lax.axis_index("lat") == lats - 1).astype(jnp.int32).reshape(1)
    low, high, weight, proj = relative_bias(flag, table, qkv_weight, proj_weight)
    rows = 3 * width // total
    staged = total % 32 == 0 and 3 * width % total == 0 and rows % 16 == 0
    if staged:
        far = total // 8
        blocks = tuple(
            (core + 2 * (k if core else PLANE[k]) + 8 * line, core + 2 * (PLANE[k] if core else k) + 8 * line)
            for core in range(2)
            for k in range(4)
            for line in line_order(far)
        )
    else:
        blocks = None
    gain = norm_gain.reshape(1, width)
    grad_qkv, unit, inverse, grad, *weight_grads = window_backward(
        place.astype(jnp.int32).reshape(1),
        quarters,
        gain,
        weight,
        proj,
        low,
        high,
        blocks,
    )
    own, to_lon, to_side = norm_backward(grad_qkv, weight, gain, unit, inverse, grad)
    factor = 1.0 / math.sqrt(span_lon * lons * span_lat * lats)
    if staged:
        keep, send = weight_grads
        keep, to_lon, to_side = lax.optimization_barrier((keep, to_lon, to_side))
        shape = (4, far, rows, width)
        pair = add_slots(keep.reshape(shape), [exchange(send.reshape(shape), 1, 1, total)]).astype(BF16)
        planes = [(2 * PLANE[k], 2 * k) for k in range(1, 4)]
        plane = add_slots(pair[0], send_slots(pair, planes, total)).astype(BF16)
        arrived = send_slots(plane, [(8 * k, 8 * k) for k in line_order(far)[1:]], total)
        summed = add_slots(plane[0], arrived).reshape(-1)
    else:
        summed = lax.psum_scatter(
            weight_grads[0].reshape(-1), AXES, scatter_dimension=0, tiled=True
        )
    from_side = lax.ppermute(to_side, AXES, route(0, 1))
    from_lon = lax.ppermute(jnp.stack([to_lon, from_side[1]]), AXES, route(-1, 0))
    token_grad = unpack(from_lon, from_side, own)
    return (token_grad, summed * factor)


def solution(mesh):
    placed = (P("lon", "lat", None), P(), P(), P(), P(), P("lon", "lat", None))
    return jax.shard_map(
        shards,
        mesh=mesh,
        in_specs=placed,
        out_specs=(P("lon", "lat", None), P(("lon", "lat"))),
        check_vma=False,
    )
```

```python
import functools
import math

import jax
import jax.numpy as jnp
from jax import lax
from jax.experimental import pallas as pl
from jax.experimental.pallas import tpu as pltpu
from jax.sharding import PartitionSpec as P

WIN = 12
EDGE = WIN // 2
AREA = WIN * WIN
QUARTER = EDGE * EDGE
SPAN = 2 * WIN - 1
LANES = 128
F32 = jnp.float32
BF16 = jnp.bfloat16
AXES = ("lon", "lat")
PLANE = (0, 2, 1, 3)


def line_order(far):
    return [0] + sorted(range(1, far), key=lambda k: (k != far // 2, k))


def dot(a, b, ca, cb):
    return lax.dot_general(a, b, (((ca,), (cb,)), ((), ())), preferred_element_type=F32)


def pack_kernel(
    tokens_hbm, grad_hbm, table_hbm, own_ref, lon_ref, lat_ref, diag_ref, table_ref, here_ref, stage_ref, sems
):
    copies = [
        pltpu.make_async_copy(tokens_hbm, here_ref.at[0], sems.at[0]),
        pltpu.make_async_copy(grad_hbm, here_ref.at[1], sems.at[1]),
        pltpu.make_async_copy(table_hbm, table_ref, sems.at[2]),
    ]
    for copy in copies:
        copy.start()
    for k in range(2):
        copies[k].wait()
        for u in range(WIN):
            line = here_ref[k, u].astype(F32)
            row = u % EDGE * EDGE
            early = u < EDGE
            row += k * QUARTER
            stage_ref[2 if early else 3, row : row + EDGE, :] = line[:EDGE]
            stage_ref[0 if early else 1, row : row + EDGE, :] = line[EDGE:]
    for n, out in enumerate((own_ref, lon_ref, lat_ref, diag_ref)):
        out[...] = stage_ref[n].astype(BF16)
    copies[2].wait()


def pack(tokens, grad, table):
    width = tokens.shape[2]
    shape = jax.ShapeDtypeStruct((2 * QUARTER, width), BF16)
    hbm = pl.BlockSpec(memory_space=pltpu.HBM)
    vmem = pl.BlockSpec(memory_space=pltpu.VMEM)
    return pl.pallas_call(
        pack_kernel,
        out_shape=(shape,) * 4 + (jax.ShapeDtypeStruct(table.shape, F32),),
        in_specs=[hbm] * 3,
        out_specs=(vmem,) * 5,
        scratch_shapes=[
            pltpu.VMEM((2,) + tokens.shape, BF16),
            pltpu.VMEM((4, 2 * QUARTER, width), F32),
            pltpu.SemaphoreType.DMA((3,)),
        ],
        compiler_params=pltpu.CompilerParams(vmem_limit_bytes=8 << 20),
        cost_estimate=pl.CostEstimate(flops=0, bytes_accessed=1 << 20, transcendentals=0),
        name="pack",
    )(*(pltpu.with_memory_space_constraint(x, pltpu.HBM) for x in (tokens, grad, table)))


def bias_kernel(
    flag_ref, table_ref, weight_hbm, proj_hbm, low_ref, high_ref, weight_ref, proj_ref, pad_ref, sems
):
    copies = []
    for source, target, chunks in ((weight_hbm, weight_ref, 6), (proj_hbm, proj_ref, 2)):
        step = source.shape[1] // chunks
        for k in range(chunks):
            part = pl.ds(k * step, step)
            copies.append(
                pltpu.make_async_copy(source.at[:, part], target.at[:, part], sems.at[len(copies)])
            )
    for copy in copies:
        copy.start()
    heads, count = table_ref.shape
    width = pad_ref.shape[1]
    pad_ref[...] = jnp.zeros_like(pad_ref)
    pad_ref[:, :count] = table_ref[...]
    flat = pad_ref[...]
    shifts = WIN + EDGE
    moved = jnp.concatenate(
        [flat] + [pltpu.roll(flat, width - b, 1) for b in range(1, shifts)], axis=0
    )
    row = lax.broadcasted_iota(jnp.int32, (width, 2 * LANES), 0)
    col = lax.broadcasted_iota(jnp.int32, (width, 2 * LANES), 1)
    place = col + (SPAN - EDGE) * ((col * 10923) >> 16)
    pick = jnp.where((row == place) & (col < SPAN * EDGE), 1.0, 0.0).astype(BF16)
    first = moved.astype(BF16)
    rest = moved - first.astype(F32)
    second = rest.astype(BF16)
    third = (rest - second.astype(F32)).astype(BF16)
    packed = dot(first, pick, 1, 0) + (dot(second, pick, 1, 0) + dot(third, pick, 1, 0))
    half = WIN * EDGE
    lane = lax.broadcasted_iota(jnp.int32, (heads, LANES), 1)
    apart = jnp.where(flag_ref[0] > 0, -1e30, 0.0).astype(F32)
    for v in range(WIN):
        b = WIN - 1 - v
        side, inner = divmod(v, EDGE)
        near = packed[heads * b : heads * (b + 1)] + (apart if side == 1 else 0.0)
        far = packed[heads * (b + EDGE) : heads * (b + EDGE + 1)] + (apart if side == 0 else 0.0)
        for u in range(WIN):
            a = EDGE * (WIN - 1 - u)
            left = pltpu.roll(near, (2 * LANES - a) % (2 * LANES), 1) if a else near
            right = pltpu.roll(far, (half - a) % (2 * LANES), 1)
            start = heads * (side * half + u * EDGE + inner)
            low_ref[start : start + heads, :] = jnp.where(
                lane < half, left[:, :LANES], right[:, :LANES]
            )
            high_ref[start : start + heads, :] = right[:, LANES:]
    for copy in copies:
        copy.wait()


def relative_bias(flag, table, weight, proj):
    heads = table.shape[0]
    shape = jax.ShapeDtypeStruct((AREA * heads, LANES), F32)
    width = -(-table.shape[1] // LANES) * LANES
    hbm = pl.BlockSpec(memory_space=pltpu.HBM)
    vmem = pl.BlockSpec(memory_space=pltpu.VMEM)
    return pl.pallas_call(
        bias_kernel,
        out_shape=(
            shape,
            shape,
            jax.ShapeDtypeStruct(weight.shape, BF16),
            jax.ShapeDtypeStruct(proj.shape, BF16),
        ),
        in_specs=[pl.BlockSpec(memory_space=pltpu.SMEM), vmem, hbm, hbm],
        out_specs=(vmem,) * 4,
        scratch_shapes=[pltpu.VMEM((heads, width), F32), pltpu.SemaphoreType.DMA((8,))],
        compiler_params=pltpu.CompilerParams(vmem_limit_bytes=16 << 20),
        cost_estimate=pl.CostEstimate(
            flops=6 * 18 * heads * width * 256, bytes_accessed=6 << 20, transcendentals=0
        ),
        name="relative_bias",
    )(flag, table, *(pltpu.with_memory_space_constraint(x, pltpu.HBM) for x in (weight, proj)))


def window_kernel(
    blocks,
    order_ref,
    own_ref,
    lon_ref,
    diag_ref,
    lat_ref,
    gain_ref,
    weight_ref,
    proj_ref,
    low_ref,
    high_ref,
    qkv_ref,
    unit_ref,
    inverse_ref,
    grad_ref,
    *rest,
):
    weight_outs = rest[:-3]
    token_ref, turned_ref, placed_ref = rest[-3:]
    width = gain_ref.shape[1]
    heads = low_ref.shape[0] // AREA
    size = width // heads
    group = LANES // size
    factor = size ** (-0.5)
    for k, ref in enumerate((lon_ref, own_ref, diag_ref, lat_ref)):
        both = ref[...].astype(F32)
        token_ref[QUARTER * k : QUARTER * (k + 1), :] = both[:QUARTER]
        grad_ref[QUARTER * k : QUARTER * (k + 1), :] = both[QUARTER:]
    inputs = token_ref[...]
    gain = gain_ref[...]
    centred = inputs - jnp.mean(inputs, axis=-1, keepdims=True)
    inverse = lax.rsqrt(jnp.mean(centred * centred, axis=-1, keepdims=True) + 1e-05)
    unit = centred * inverse
    unit_ref[...] = unit
    inverse_ref[...] = jnp.broadcast_to(inverse, inverse_ref.shape)
    normed = (unit * gain).astype(BF16)
    qkv_ref[...] = dot(normed, weight_ref[...], 1, 0).astype(BF16)
    upstream = dot(grad_ref[...].astype(BF16), proj_ref[...], 1, 1).astype(BF16)
    lane = lax.broadcasted_iota(jnp.int32, (AREA, LANES), 1)
    zero = jnp.zeros((AREA, LANES), BF16)
    here = [(lane >= size * n) & (lane < size * (n + 1)) for n in range(group)]
    left = AREA - LANES
    packed = LANES // left
    span = packed * size
    row = lax.broadcasted_iota(jnp.int32, (LANES, span), 0)
    col = lax.broadcasted_iota(jnp.int32, (LANES, span), 1)
    own_block = row // left == col // size

    def diagonal(block):
        return jnp.where(own_block, jnp.concatenate([block] * packed, axis=0), jnp.zeros((LANES, span), BF16))

    def attend(scores, grad_probs, bias):
        scores = scores * factor + bias
        weights = jnp.exp(scores - jnp.max(scores, axis=0, keepdims=True))
        probs = weights * (1.0 / jnp.sum(weights, axis=0, keepdims=True))
        centre = jnp.sum(probs * grad_probs, axis=0, keepdims=True)
        return probs.astype(BF16), (probs * (grad_probs - centre) * factor).astype(BF16)

    for f in range(width // span):
        base = span * f
        query_all = qkv_ref[:, base : base + span]
        keys_all = qkv_ref[:, width + base : width + base + span]
        values_all = qkv_ref[:, 2 * width + base : 2 * width + base + span]
        up_all = upstream[:, base : base + span]
        keys_turned = keys_all.T
        query_left = diagonal(query_all[LANES:])
        up_left = diagonal(up_all[LANES:])
        bias = None
        for n in range(packed):
            part = high_ref[pl.ds(f * packed + n, AREA, stride=heads), :]
            if n == 0:
                bias = part
            else:
                bias = jnp.where(lane >= left * n, pltpu.roll(part, left * n, 1), bias)
        probs, grad_scores = attend(
            dot(keys_all, query_left, 1, 1), dot(values_all, up_left, 1, 1), bias
        )
        left_values = dot(probs, up_left, 1, 0)
        left_keys = dot(grad_scores, query_left, 1, 0)
        left_query = dot(keys_turned, grad_scores, 1, 0)
        for n in range(packed):
            part = left_query[size * n : size * (n + 1)]
            if n:
                part = pltpu.roll(part, LANES - left * n, 1)
            turned_ref[base + size * n : base + size * (n + 1), LANES:] = part[:, :left].astype(BF16)
        for g in range(span // LANES):
            inner = slice(LANES * g, LANES * (g + 1))
            start = base + LANES * g
            query = query_all[:LANES, inner]
            keys = keys_all[:, inner]
            values = values_all[:, inner]
            up = up_all[:LANES, inner]
            all_scores = dot(
                jnp.concatenate([jnp.where(m, keys, zero) for m in here], axis=0), query, 1, 1
            )
            all_grads = dot(
                jnp.concatenate([jnp.where(m, values, zero) for m in here], axis=0), up, 1, 1
            )
            low_probs, low_scores = [], []
            for n in range(group):
                first = start + size * n
                rows = slice(AREA * n, AREA * (n + 1))
                bias = low_ref[pl.ds(first // size, AREA, stride=heads), :]
                probs, grad_scores = attend(all_scores[rows], all_grads[rows], bias)
                low_probs.append(probs)
                low_scores.append(grad_scores)
                part = dot(keys_turned[LANES * g + size * n : LANES * g + size * (n + 1)], grad_scores, 1, 0)
                turned_ref[first : first + size, :LANES] = part.astype(BF16)
            all_values = dot(jnp.concatenate(low_probs, axis=0), up, 1, 0)
            all_keys = dot(jnp.concatenate(low_scores, axis=0), query, 1, 0)
            grad_values, grad_keys = all_values[:AREA], all_keys[:AREA]
            for n in range(1, group):
                rows = slice(AREA * n, AREA * (n + 1))
                grad_values = jnp.where(here[n], all_values[rows], grad_values)
                grad_keys = jnp.where(here[n], all_keys[rows], grad_keys)
            grad_values = (grad_values + left_values[:, inner]).astype(BF16)
            grad_keys = (grad_keys + left_keys[:, inner]).astype(BF16)
            qkv_ref[:, start : start + LANES] = turned_ref[start : start + LANES, :].T
            qkv_ref[:, width + start : width + start + LANES] = grad_keys
            qkv_ref[:, 2 * width + start : 2 * width + start + LANES] = grad_values
            turned_ref[width + start : width + start + LANES, :] = grad_keys.T
            turned_ref[2 * width + start : 2 * width + start + LANES, :] = grad_values.T
    if blocks is None:
        weight_outs[0][...] = dot(turned_ref[...], normed, 1, 0)
    else:
        rows = 3 * width // len(blocks)
        place = order_ref[0]
        odd = place % 2 == 1
        for slot, (even_offset, odd_offset) in enumerate(blocks):
            offset = jnp.where(odd, odd_offset, even_offset)
            start = pl.multiple_of((place ^ offset) * rows, rows)
            placed_ref[slot * rows : (slot + 1) * rows, :] = turned_ref[pl.ds(start, rows), :]
        total = 3 * width // len(weight_outs)
        for k, ref in enumerate(weight_outs):
            ref[...] = dot(placed_ref[total * k : total * (k + 1), :], normed, 1, 0).astype(BF16)


def window_backward(order, quarters, gain, weight, proj, low, high, blocks):
    width = proj.shape[0]
    if blocks is None:
        weight_shapes = (jax.ShapeDtypeStruct((3 * width, width), F32),)
    else:
        weight_shapes = (jax.ShapeDtypeStruct((3 * width // 2, width), BF16),) * 2
    vmem = pl.BlockSpec(memory_space=pltpu.VMEM)
    return pl.pallas_call(
        functools.partial(window_kernel, blocks),
        out_shape=(
            jax.ShapeDtypeStruct((AREA, 3 * width), BF16),
            jax.ShapeDtypeStruct((AREA, width), F32),
            jax.ShapeDtypeStruct((AREA, LANES), F32),
            jax.ShapeDtypeStruct((AREA, width), F32),
        )
        + weight_shapes,
        in_specs=[pl.BlockSpec(memory_space=pltpu.SMEM)] + [vmem] * 9,
        out_specs=(vmem,) * (4 + len(weight_shapes)),
        scratch_shapes=[
            pltpu.VMEM((AREA, width), F32),
            pltpu.VMEM((3 * width, AREA), BF16),
            pltpu.VMEM((3 * width, AREA), BF16),
        ],
        compiler_params=pltpu.CompilerParams(vmem_limit_bytes=32 << 20),
        cost_estimate=pl.CostEstimate(
            flops=2 * AREA * width * width * 7, bytes_accessed=6 << 20, transcendentals=16 * AREA * AREA
        ),
        name="window_backward",
    )(order, *quarters, gain, weight, proj, low, high)


def norm_kernel(
    qkv_ref, weight_ref, gain_ref, unit_ref, inverse_ref, grad_ref, own_out, lon_out, side_out, token_ref
):
    unit = unit_ref[...]
    scaled = dot(qkv_ref[...], weight_ref[...], 1, 1) * gain_ref[...]
    result = grad_ref[...] + inverse_ref[:, :1] * (
        scaled
        - jnp.mean(scaled, axis=-1, keepdims=True)
        - unit * jnp.mean(scaled * unit, axis=-1, keepdims=True)
    )
    token_ref[...] = result
    for k, ref in enumerate((lon_out, own_out, side_out.at[1], side_out.at[0])):
        ref[...] = token_ref[QUARTER * k : QUARTER * (k + 1), :].astype(BF16)


def norm_backward(qkv, weight, gain, unit, inverse, grad):
    width = unit.shape[1]
    piece = jax.ShapeDtypeStruct((QUARTER, width), BF16)
    vmem = pl.BlockSpec(memory_space=pltpu.VMEM)
    return pl.pallas_call(
        norm_kernel,
        out_shape=(piece, piece, jax.ShapeDtypeStruct((2, QUARTER, width), BF16)),
        in_specs=[vmem] * 6,
        out_specs=(vmem,) * 3,
        scratch_shapes=[pltpu.VMEM((AREA, width), F32)],
        compiler_params=pltpu.CompilerParams(vmem_limit_bytes=16 << 20),
        cost_estimate=pl.CostEstimate(
            flops=6 * AREA * width * width, bytes_accessed=3 << 20, transcendentals=0
        ),
        name="norm_backward",
    )(qkv, weight, gain, unit, inverse, grad)


def unpack_kernel(lon_ref, side_ref, own_ref, out_ref, line_ref):
    for u in range(WIN):
        left, right = (side_ref[0], own_ref[...]) if u < EDGE else (lon_ref[1], lon_ref[0])
        rows = slice(u % EDGE * EDGE, u % EDGE * EDGE + EDGE)
        line_ref[u, :EDGE, :] = left.astype(F32)[rows]
        line_ref[u, EDGE:, :] = right.astype(F32)[rows]
    out_ref[...] = line_ref[...].astype(BF16)


def unpack(lon, side, own):
    width = own.shape[1]
    vmem = pl.BlockSpec(memory_space=pltpu.VMEM)
    return pl.pallas_call(
        unpack_kernel,
        out_shape=jax.ShapeDtypeStruct((WIN, WIN, width), BF16),
        in_specs=[vmem] * 3,
        out_specs=vmem,
        scratch_shapes=[pltpu.VMEM((WIN, WIN, width), F32)],
        compiler_params=pltpu.CompilerParams(vmem_limit_bytes=8 << 20),
        cost_estimate=pl.CostEstimate(flops=0, bytes_accessed=1 << 19, transcendentals=0),
        name="unpack",
    )(lon, side, own)


def exchange(block, even, odd, total):
    pairs = [(i, i ^ (odd if i % 2 else even)) for i in range(total)]
    return lax.ppermute(block, AXES, pairs)


def send_slots(slots, offsets, total):
    return [exchange(slots[k + 1], *offset, total) for k, offset in enumerate(offsets)]


def add_slots(own, arrived):
    summed = own.astype(F32)
    for piece in arrived:
        summed = summed + piece.astype(F32)
    return summed


def shards(tokens, norm_gain, qkv_weight, bias_table, proj_weight, out_grad):
    span_lon, span_lat, width = tokens.shape
    lons, lats = lax.axis_size("lon"), lax.axis_size("lat")
    total = lons * lats
    place = lax.axis_index("lon") * lats + lax.axis_index("lat")

    def route(step_lon, step_lat):
        return [
            (a * lats + b, (a + step_lon) % lons * lats + (b + step_lat) % lats)
            for a in range(lons)
            for b in range(lats)
        ]

    own, lon_start, lat_start, diag_start, table = pack(tokens, out_grad, bias_table)
    at_lon = lax.ppermute(lon_start, AXES, route(1, 0))
    at_diag = lax.ppermute(diag_start, AXES, route(1, -1))
    at_lat = lax.ppermute(lat_start, AXES, route(0, -1))
    quarters = [own, at_lon, at_diag, at_lat]
    flag = (lax.axis_index("lat") == lats - 1).astype(jnp.int32).reshape(1)
    low, high, weight, proj = relative_bias(flag, table, qkv_weight, proj_weight)
    rows = 3 * width // total
    staged = total % 32 == 0 and 3 * width % total == 0 and rows % 16 == 0
    if staged:
        far = total // 8
        blocks = tuple(
            (core + 2 * (k if core else PLANE[k]) + 8 * line, core + 2 * (PLANE[k] if core else k) + 8 * line)
            for core in range(2)
            for k in range(4)
            for line in line_order(far)
        )
    else:
        blocks = None
    gain = norm_gain.reshape(1, width)
    grad_qkv, unit, inverse, grad, *weight_grads = window_backward(
        place.astype(jnp.int32).reshape(1),
        quarters,
        gain,
        weight,
        proj,
        low,
        high,
        blocks,
    )
    own, to_lon, to_side = norm_backward(grad_qkv, weight, gain, unit, inverse, grad)
    factor = 1.0 / math.sqrt(span_lon * lons * span_lat * lats)
    if staged:
        keep, send = weight_grads
        keep, to_lon, to_side = lax.optimization_barrier((keep, to_lon, to_side))
        shape = (4, far, rows, width)
        pair = add_slots(keep.reshape(shape), [exchange(send.reshape(shape), 1, 1, total)]).astype(BF16)
        planes = [(2 * PLANE[k], 2 * k) for k in range(1, 4)]
        plane = add_slots(pair[0], send_slots(pair, planes, total)).astype(BF16)
        arrived = send_slots(plane, [(8 * k, 8 * k) for k in line_order(far)[1:]], total)
        summed = add_slots(plane[0], arrived).reshape(-1)
    else:
        summed = lax.psum_scatter(
            weight_grads[0].reshape(-1), AXES, scatter_dimension=0, tiled=True
        )
    from_side = lax.ppermute(to_side, AXES, route(0, 1))
    from_lon = lax.ppermute(jnp.stack([to_lon, from_side[1]]), AXES, route(-1, 0))
    token_grad = unpack(from_lon, from_side, own)
    return (token_grad, summed * factor)


def solution(mesh):
    placed = (P("lon", "lat", None), P(), P(), P(), P(), P("lon", "lat", None))
    return jax.shard_map(
        shards,
        mesh=mesh,
        in_specs=placed,
        out_specs=(P("lon", "lat", None), P(("lon", "lat"))),
        check_vma=False,
    )
```

```python
import functools
import math

import jax
import jax.numpy as jnp
from jax import lax
from jax.experimental import pallas as pl
from jax.experimental.pallas import tpu as pltpu
from jax.sharding import PartitionSpec as P

WIN = 12
EDGE = WIN // 2
AREA = WIN * WIN
QUARTER = EDGE * EDGE
SPAN = 2 * WIN - 1
LANES = 128
F32 = jnp.float32
BF16 = jnp.bfloat16
ROOM = 8
AXES = ("lon", "lat")
PLANE = (0, 2, 1, 3)


def line_order(far):
    return [0] + sorted(range(1, far), key=lambda k: (k != far // 2, k))


def dot(a, b, ca, cb):
    return lax.dot_general(a, b, (((ca,), (cb,)), ((), ())), preferred_element_type=F32)


def pack_kernel(
    tokens_hbm, grad_hbm, table_hbm, own_ref, lon_ref, lat_ref, diag_ref, table_ref, here_ref, stage_ref, sems
):
    copies = [
        pltpu.make_async_copy(tokens_hbm, here_ref.at[0], sems.at[0]),
        pltpu.make_async_copy(grad_hbm, here_ref.at[1], sems.at[1]),
        pltpu.make_async_copy(table_hbm, table_ref, sems.at[2]),
    ]
    for copy in copies:
        copy.start()
    for k in range(2):
        copies[k].wait()
        for u in range(WIN):
            line = here_ref[k, u].astype(F32)
            row = u % EDGE * EDGE
            early = u < EDGE
            row += k * QUARTER
            stage_ref[2 if early else 3, row : row + EDGE, :] = line[:EDGE]
            stage_ref[0 if early else 1, row : row + EDGE, :] = line[EDGE:]
    for n, out in enumerate((own_ref, lon_ref, lat_ref, diag_ref)):
        out[...] = stage_ref[n, : 2 * QUARTER, :].astype(BF16)
    copies[2].wait()


def pack(tokens, grad, table):
    width = tokens.shape[2]
    shape = jax.ShapeDtypeStruct((2 * QUARTER, width), BF16)
    hbm = pl.BlockSpec(memory_space=pltpu.HBM)
    vmem = pl.BlockSpec(memory_space=pltpu.VMEM)
    return pl.pallas_call(
        pack_kernel,
        out_shape=(shape,) * 4 + (jax.ShapeDtypeStruct(table.shape, F32),),
        in_specs=[hbm] * 3,
        out_specs=(vmem,) * 5,
        scratch_shapes=[
            pltpu.VMEM((2,) + tokens.shape, BF16),
            pltpu.VMEM((4, 2 * QUARTER + ROOM, width), F32),
            pltpu.SemaphoreType.DMA((3,)),
        ],
        compiler_params=pltpu.CompilerParams(vmem_limit_bytes=8 << 20),
        cost_estimate=pl.CostEstimate(flops=0, bytes_accessed=1 << 20, transcendentals=0),
        name="pack",
    )(*(pltpu.with_memory_space_constraint(x, pltpu.HBM) for x in (tokens, grad, table)))


def bias_kernel(
    flag_ref, table_ref, weight_hbm, proj_hbm, low_ref, high_ref, weight_ref, proj_ref, pad_ref, sems
):
    copies = []
    for source, target, chunks in ((weight_hbm, weight_ref, 6), (proj_hbm, proj_ref, 2)):
        step = source.shape[1] // chunks
        for k in range(chunks):
            part = pl.ds(k * step, step)
            copies.append(
                pltpu.make_async_copy(source.at[:, part], target.at[:, part], sems.at[len(copies)])
            )
    for copy in copies:
        copy.start()
    heads, count = table_ref.shape
    width = pad_ref.shape[1]
    pad_ref[...] = jnp.zeros_like(pad_ref)
    pad_ref[:, :count] = table_ref[...]
    flat = pad_ref[...]
    shifts = WIN + EDGE
    moved = jnp.concatenate(
        [flat] + [pltpu.roll(flat, width - b, 1) for b in range(1, shifts)], axis=0
    )
    row = lax.broadcasted_iota(jnp.int32, (width, 2 * LANES), 0)
    col = lax.broadcasted_iota(jnp.int32, (width, 2 * LANES), 1)
    place = col + (SPAN - EDGE) * ((col * 10923) >> 16)
    pick = jnp.where((row == place) & (col < SPAN * EDGE), 1.0, 0.0).astype(BF16)
    first = moved.astype(BF16)
    rest = moved - first.astype(F32)
    second = rest.astype(BF16)
    third = (rest - second.astype(F32)).astype(BF16)
    packed = dot(first, pick, 1, 0) + (dot(second, pick, 1, 0) + dot(third, pick, 1, 0))
    half = WIN * EDGE
    lane = lax.broadcasted_iota(jnp.int32, (heads, LANES), 1)
    apart = jnp.where(flag_ref[0] > 0, -1e30, 0.0).astype(F32)
    for v in range(WIN):
        b = WIN - 1 - v
        side, inner = divmod(v, EDGE)
        near = packed[heads * b : heads * (b + 1)] + (apart if side == 1 else 0.0)
        far = packed[heads * (b + EDGE) : heads * (b + EDGE + 1)] + (apart if side == 0 else 0.0)
        for u in range(WIN):
            a = EDGE * (WIN - 1 - u)
            left = pltpu.roll(near, (2 * LANES - a) % (2 * LANES), 1) if a else near
            right = pltpu.roll(far, (half - a) % (2 * LANES), 1)
            start = heads * (side * half + u * EDGE + inner)
            low_ref[start : start + heads, :] = jnp.where(
                lane < half, left[:, :LANES], right[:, :LANES]
            )
            high_ref[start : start + heads, :] = right[:, LANES:]
    for copy in copies:
        copy.wait()


def relative_bias(flag, table, weight, proj):
    heads = table.shape[0]
    shape = jax.ShapeDtypeStruct((AREA * heads, LANES), F32)
    width = -(-table.shape[1] // LANES) * LANES
    hbm = pl.BlockSpec(memory_space=pltpu.HBM)
    vmem = pl.BlockSpec(memory_space=pltpu.VMEM)
    return pl.pallas_call(
        bias_kernel,
        out_shape=(
            shape,
            shape,
            jax.ShapeDtypeStruct(weight.shape, BF16),
            jax.ShapeDtypeStruct(proj.shape, BF16),
        ),
        in_specs=[pl.BlockSpec(memory_space=pltpu.SMEM), vmem, hbm, hbm],
        out_specs=(vmem,) * 4,
        scratch_shapes=[pltpu.VMEM((heads, width), F32), pltpu.SemaphoreType.DMA((8,))],
        compiler_params=pltpu.CompilerParams(vmem_limit_bytes=16 << 20),
        cost_estimate=pl.CostEstimate(
            flops=6 * 18 * heads * width * 256, bytes_accessed=6 << 20, transcendentals=0
        ),
        name="relative_bias",
    )(flag, table, *(pltpu.with_memory_space_constraint(x, pltpu.HBM) for x in (weight, proj)))


def window_kernel(
    blocks,
    order_ref,
    own_ref,
    lon_ref,
    diag_ref,
    lat_ref,
    gain_ref,
    weight_ref,
    proj_ref,
    low_ref,
    high_ref,
    qkv_ref,
    unit_ref,
    inverse_ref,
    grad_ref,
    *rest,
):
    weight_outs = rest[:-3]
    token_ref, turned_ref, placed_ref = rest[-3:]
    width = gain_ref.shape[1]
    heads = low_ref.shape[0] // AREA
    size = width // heads
    group = LANES // size
    factor = size ** (-0.5)
    for k, ref in enumerate((lon_ref, own_ref, diag_ref, lat_ref)):
        both = ref[...].astype(F32)
        token_ref[QUARTER * k : QUARTER * (k + 1), :] = both[:QUARTER]
        grad_ref[QUARTER * k : QUARTER * (k + 1), :] = both[QUARTER:]
    inputs = token_ref[:AREA, :]
    gain = gain_ref[...]
    centred = inputs - jnp.mean(inputs, axis=-1, keepdims=True)
    inverse = lax.rsqrt(jnp.mean(centred * centred, axis=-1, keepdims=True) + 1e-05)
    unit = centred * inverse
    unit_ref[...] = unit
    inverse_ref[...] = jnp.broadcast_to(inverse, inverse_ref.shape)
    normed = (unit * gain).astype(BF16)
    qkv_ref[...] = dot(normed, weight_ref[...], 1, 0).astype(BF16)
    upstream = dot(grad_ref[:AREA, :].astype(BF16), proj_ref[...], 1, 1).astype(BF16)
    lane = lax.broadcasted_iota(jnp.int32, (AREA, LANES), 1)
    zero = jnp.zeros((AREA, LANES), BF16)
    here = [(lane >= size * n) & (lane < size * (n + 1)) for n in range(group)]
    left = AREA - LANES
    packed = LANES // left
    span = packed * size
    row = lax.broadcasted_iota(jnp.int32, (LANES, span), 0)
    col = lax.broadcasted_iota(jnp.int32, (LANES, span), 1)
    own_block = row // left == col // size

    def diagonal(block):
        return jnp.where(own_block, jnp.concatenate([block] * packed, axis=0), jnp.zeros((LANES, span), BF16))

    def attend(scores, grad_probs, bias):
        scores = scores * factor + bias
        weights = jnp.exp(scores - jnp.max(scores, axis=0, keepdims=True))
        probs = weights * (1.0 / jnp.sum(weights, axis=0, keepdims=True))
        centre = jnp.sum(probs * grad_probs, axis=0, keepdims=True)
        return probs.astype(BF16), (probs * (grad_probs - centre) * factor).astype(BF16)

    for f in range(width // span):
        base = span * f
        query_all = qkv_ref[:, base : base + span]
        keys_all = qkv_ref[:, width + base : width + base + span]
        values_all = qkv_ref[:, 2 * width + base : 2 * width + base + span]
        up_all = upstream[:, base : base + span]
        keys_turned = keys_all.T
        query_left = diagonal(query_all[LANES:])
        up_left = diagonal(up_all[LANES:])
        bias = None
        for n in range(packed):
            part = high_ref[pl.ds(f * packed + n, AREA, stride=heads), :]
            if n == 0:
                bias = part
            else:
                bias = jnp.where(lane >= left * n, pltpu.roll(part, left * n, 1), bias)
        probs, grad_scores = attend(
            dot(keys_all, query_left, 1, 1), dot(values_all, up_left, 1, 1), bias
        )
        left_values = dot(probs, up_left, 1, 0)
        left_keys = dot(grad_scores, query_left, 1, 0)
        left_query = dot(keys_turned, grad_scores, 1, 0)
        for n in range(packed):
            part = left_query[size * n : size * (n + 1)]
            if n:
                part = pltpu.roll(part, LANES - left * n, 1)
            turned_ref[base + size * n : base + size * (n + 1), LANES:] = part[:, :left].astype(BF16)
        for g in range(span // LANES):
            inner = slice(LANES * g, LANES * (g + 1))
            start = base + LANES * g
            query = query_all[:LANES, inner]
            keys = keys_all[:, inner]
            values = values_all[:, inner]
            up = up_all[:LANES, inner]
            all_scores = dot(
                jnp.concatenate([jnp.where(m, keys, zero) for m in here], axis=0), query, 1, 1
            )
            all_grads = dot(
                jnp.concatenate([jnp.where(m, values, zero) for m in here], axis=0), up, 1, 1
            )
            low_probs, low_scores = [], []
            for n in range(group):
                first = start + size * n
                rows = slice(AREA * n, AREA * (n + 1))
                bias = low_ref[pl.ds(first // size, AREA, stride=heads), :]
                probs, grad_scores = attend(all_scores[rows], all_grads[rows], bias)
                low_probs.append(probs)
                low_scores.append(grad_scores)
                part = dot(keys_turned[LANES * g + size * n : LANES * g + size * (n + 1)], grad_scores, 1, 0)
                turned_ref[first : first + size, :LANES] = part.astype(BF16)
            all_values = dot(jnp.concatenate(low_probs, axis=0), up, 1, 0)
            all_keys = dot(jnp.concatenate(low_scores, axis=0), query, 1, 0)
            grad_values, grad_keys = all_values[:AREA], all_keys[:AREA]
            for n in range(1, group):
                rows = slice(AREA * n, AREA * (n + 1))
                grad_values = jnp.where(here[n], all_values[rows], grad_values)
                grad_keys = jnp.where(here[n], all_keys[rows], grad_keys)
            grad_values = (grad_values + left_values[:, inner]).astype(BF16)
            grad_keys = (grad_keys + left_keys[:, inner]).astype(BF16)
            qkv_ref[:, start : start + LANES] = turned_ref[start : start + LANES, :].T
            qkv_ref[:, width + start : width + start + LANES] = grad_keys
            qkv_ref[:, 2 * width + start : 2 * width + start + LANES] = grad_values
            turned_ref[width + start : width + start + LANES, :] = grad_keys.T
            turned_ref[2 * width + start : 2 * width + start + LANES, :] = grad_values.T
    if blocks is None:
        weight_outs[0][...] = dot(turned_ref[...], normed, 1, 0)
    else:
        send_ref, kept_ref, normed_ref = weight_outs
        rows = 3 * width // len(blocks)
        half = 3 * width // 2
        place = order_ref[0]
        odd = place % 2 == 1
        for slot, (even_offset, odd_offset) in enumerate(blocks):
            offset = jnp.where(odd, odd_offset, even_offset)
            start = pl.multiple_of((place ^ offset) * rows, rows)
            target, first = (kept_ref, slot * rows) if slot * rows < half else (placed_ref, slot * rows - half)
            target[first : first + rows, :] = turned_ref[pl.ds(start, rows), :]
        send_ref[...] = dot(placed_ref[...], normed, 1, 0).astype(BF16)
        normed_ref[...] = normed


def window_backward(order, quarters, gain, weight, proj, low, high, blocks):
    width = proj.shape[0]
    if blocks is None:
        weight_shapes = (jax.ShapeDtypeStruct((3 * width, width), F32),)
    else:
        weight_shapes = (
            jax.ShapeDtypeStruct((3 * width // 2, width), BF16),
            jax.ShapeDtypeStruct((3 * width // 2, AREA), BF16),
            jax.ShapeDtypeStruct((AREA, width), BF16),
        )
    vmem = pl.BlockSpec(memory_space=pltpu.VMEM)
    return pl.pallas_call(
        functools.partial(window_kernel, blocks),
        out_shape=(
            jax.ShapeDtypeStruct((AREA, 3 * width), BF16),
            jax.ShapeDtypeStruct((AREA, width), F32),
            jax.ShapeDtypeStruct((AREA, LANES), F32),
            jax.ShapeDtypeStruct((AREA + ROOM, width), F32),
        )
        + weight_shapes,
        in_specs=[pl.BlockSpec(memory_space=pltpu.SMEM)] + [vmem] * 9,
        out_specs=(vmem,) * (4 + len(weight_shapes)),
        scratch_shapes=[
            pltpu.VMEM((AREA + ROOM, width), F32),
            pltpu.VMEM((3 * width, AREA), BF16),
            pltpu.VMEM((3 * width // 2, AREA), BF16),
        ],
        compiler_params=pltpu.CompilerParams(vmem_limit_bytes=32 << 20),
        cost_estimate=pl.CostEstimate(
            flops=2 * AREA * width * width * 7, bytes_accessed=6 << 20, transcendentals=16 * AREA * AREA
        ),
        name="window_backward",
    )(order, *quarters, gain, weight, proj, low, high)


def norm_kernel(
    qkv_ref, weight_ref, gain_ref, unit_ref, inverse_ref, grad_ref, *rest
):
    if len(rest) > 4:
        kept_ref, normed_ref, *rest = rest
        keep_out = rest.pop(3)
        keep_out[...] = dot(kept_ref[...], normed_ref[...], 1, 0).astype(BF16)
    own_out, lon_out, side_out, token_ref = rest
    unit = unit_ref[...]
    scaled = dot(qkv_ref[...], weight_ref[...], 1, 1) * gain_ref[...]
    result = grad_ref[:AREA, :] + inverse_ref[:, :1] * (
        scaled
        - jnp.mean(scaled, axis=-1, keepdims=True)
        - unit * jnp.mean(scaled * unit, axis=-1, keepdims=True)
    )
    token_ref[:AREA, :] = result
    for k, ref in enumerate((lon_out, own_out, side_out.at[1], side_out.at[0])):
        ref[...] = token_ref[QUARTER * k : QUARTER * (k + 1), :].astype(BF16)


def norm_backward(qkv, weight, gain, unit, inverse, grad, kept):
    width = unit.shape[1]
    piece = jax.ShapeDtypeStruct((QUARTER, width), BF16)
    keep = (jax.ShapeDtypeStruct((3 * width // 2, width), BF16),) if kept else ()
    vmem = pl.BlockSpec(memory_space=pltpu.VMEM)
    return pl.pallas_call(
        norm_kernel,
        out_shape=(piece, piece, jax.ShapeDtypeStruct((2, QUARTER, width), BF16)) + keep,
        in_specs=[vmem] * (6 + len(kept)),
        out_specs=(vmem,) * (3 + len(keep)),
        scratch_shapes=[pltpu.VMEM((AREA + ROOM, width), F32)],
        compiler_params=pltpu.CompilerParams(vmem_limit_bytes=16 << 20),
        cost_estimate=pl.CostEstimate(
            flops=6 * AREA * width * width, bytes_accessed=3 << 20, transcendentals=0
        ),
        name="norm_backward",
    )(qkv, weight, gain, unit, inverse, grad, *kept)


def unpack_kernel(lon_ref, side_ref, own_ref, out_ref, line_ref):
    for u in range(WIN):
        left, right = (side_ref[0], own_ref[...]) if u < EDGE else (lon_ref[1], lon_ref[0])
        rows = slice(u % EDGE * EDGE, u % EDGE * EDGE + EDGE)
        line_ref[u, :EDGE, :] = left.astype(F32)[rows]
        line_ref[u, EDGE:WIN, :] = right.astype(F32)[rows]
    out_ref[...] = line_ref[:, :WIN, :].astype(BF16)


def unpack(lon, side, own):
    width = own.shape[1]
    vmem = pl.BlockSpec(memory_space=pltpu.VMEM)
    return pl.pallas_call(
        unpack_kernel,
        out_shape=jax.ShapeDtypeStruct((WIN, WIN, width), BF16),
        in_specs=[vmem] * 3,
        out_specs=vmem,
        scratch_shapes=[pltpu.VMEM((WIN, 2 * ROOM, width), F32)],
        compiler_params=pltpu.CompilerParams(vmem_limit_bytes=8 << 20),
        cost_estimate=pl.CostEstimate(flops=0, bytes_accessed=1 << 19, transcendentals=0),
        name="unpack",
    )(lon, side, own)


def exchange(block, even, odd, total):
    pairs = [(i, i ^ (odd if i % 2 else even)) for i in range(total)]
    return lax.ppermute(block, AXES, pairs)


def send_slots(slots, offsets, total):
    return [exchange(slots[k + 1], *offset, total) for k, offset in enumerate(offsets)]


def add_slots(own, arrived):
    summed = own.astype(F32)
    for piece in arrived:
        summed = summed + piece.astype(F32)
    return summed


def shards(tokens, norm_gain, qkv_weight, bias_table, proj_weight, out_grad):
    span_lon, span_lat, width = tokens.shape
    lons, lats = lax.axis_size("lon"), lax.axis_size("lat")
    total = lons * lats
    place = lax.axis_index("lon") * lats + lax.axis_index("lat")

    def route(step_lon, step_lat):
        return [
            (a * lats + b, (a + step_lon) % lons * lats + (b + step_lat) % lats)
            for a in range(lons)
            for b in range(lats)
        ]

    own, lon_start, lat_start, diag_start, table = pack(tokens, out_grad, bias_table)
    at_lon = lax.ppermute(lon_start, AXES, route(1, 0))
    at_diag = lax.ppermute(diag_start, AXES, route(1, -1))
    at_lat = lax.ppermute(lat_start, AXES, route(0, -1))
    quarters = [own, at_lon, at_diag, at_lat]
    flag = (lax.axis_index("lat") == lats - 1).astype(jnp.int32).reshape(1)
    low, high, weight, proj = relative_bias(flag, table, qkv_weight, proj_weight)
    rows = 3 * width // total
    staged = total % 32 == 0 and 3 * width % total == 0 and rows % 16 == 0
    if staged:
        far = total // 8
        blocks = tuple(
            (core + 2 * (k if core else PLANE[k]) + 8 * line, core + 2 * (PLANE[k] if core else k) + 8 * line)
            for core in range(2)
            for k in range(4)
            for line in line_order(far)
        )
    else:
        blocks = None
    gain = norm_gain.reshape(1, width)
    grad_qkv, unit, inverse, grad, *weight_grads = window_backward(
        place.astype(jnp.int32).reshape(1),
        quarters,
        gain,
        weight,
        proj,
        low,
        high,
        blocks,
    )
    own, to_lon, to_side, *keep = norm_backward(
        grad_qkv, weight, gain, unit, inverse, grad, weight_grads[1:]
    )
    factor = 1.0 / math.sqrt(span_lon * lons * span_lat * lats)
    if staged:
        send, keep = weight_grads[0], keep[0]
        shape = (4, far, rows, width)
        pair = add_slots(keep.reshape(shape), [exchange(send.reshape(shape), 1, 1, total)]).astype(BF16)
        planes = [(2 * PLANE[k], 2 * k) for k in range(1, 4)]
        plane = add_slots(pair[0], send_slots(pair, planes, total)).astype(BF16)
        arrived = send_slots(plane, [(8 * k, 8 * k) for k in line_order(far)[1:]], total)
        summed = add_slots(plane[0], arrived).reshape(-1)
    else:
        summed = lax.psum_scatter(
            weight_grads[0].reshape(-1), AXES, scatter_dimension=0, tiled=True
        )
    from_side = lax.ppermute(to_side, AXES, route(0, 1))
    from_lon = lax.ppermute(jnp.stack([to_lon, from_side[1]]), AXES, route(-1, 0))
    token_grad = unpack(from_lon, from_side, own)
    return (token_grad, summed * factor)


def solution(mesh):
    placed = (P("lon", "lat", None), P(), P(), P(), P(), P("lon", "lat", None))
    return jax.shard_map(
        shards,
        mesh=mesh,
        in_specs=placed,
        out_specs=(P("lon", "lat", None), P(("lon", "lat"))),
        check_vma=False,
    )
```

```python
import functools
import math

import jax
import jax.numpy as jnp
from jax import lax
from jax.experimental import pallas as pl
from jax.experimental.pallas import tpu as pltpu
from jax.sharding import PartitionSpec as P

WIN = 12
EDGE = WIN // 2
AREA = WIN * WIN
QUARTER = EDGE * EDGE
SPAN = 2 * WIN - 1
LANES = 128
F32 = jnp.float32
BF16 = jnp.bfloat16
ROOM = 8
AXES = ("lon", "lat")
PLANE = (0, 2, 1, 3)


def line_order(far):
    return [0] + sorted(range(1, far), key=lambda k: (k != far // 2, k))


def dot(a, b, ca, cb):
    return lax.dot_general(a, b, (((ca,), (cb,)), ((), ())), preferred_element_type=F32)


def pack_kernel(
    tokens_hbm, grad_hbm, table_hbm, own_ref, lon_ref, lat_ref, diag_ref, table_ref, here_ref, stage_ref, sems
):
    copies = [
        pltpu.make_async_copy(tokens_hbm, here_ref.at[0], sems.at[0]),
        pltpu.make_async_copy(grad_hbm, here_ref.at[1], sems.at[1]),
        pltpu.make_async_copy(table_hbm, table_ref, sems.at[2]),
    ]
    for copy in copies:
        copy.start()
    for k in range(2):
        copies[k].wait()
        for u in range(WIN):
            line = here_ref[k, u].astype(F32)
            row = u % EDGE * EDGE
            early = u < EDGE
            row += k * QUARTER
            stage_ref[2 if early else 3, row : row + EDGE, :] = line[:EDGE]
            stage_ref[0 if early else 1, row : row + EDGE, :] = line[EDGE:]
    for n, out in enumerate((own_ref, lon_ref, lat_ref, diag_ref)):
        out[...] = stage_ref[n, : 2 * QUARTER, :].astype(BF16)
    copies[2].wait()


def pack(tokens, grad, table):
    width = tokens.shape[2]
    shape = jax.ShapeDtypeStruct((2 * QUARTER, width), BF16)
    hbm = pl.BlockSpec(memory_space=pltpu.HBM)
    vmem = pl.BlockSpec(memory_space=pltpu.VMEM)
    return pl.pallas_call(
        pack_kernel,
        out_shape=(shape,) * 4 + (jax.ShapeDtypeStruct(table.shape, F32),),
        in_specs=[hbm] * 3,
        out_specs=(vmem,) * 5,
        scratch_shapes=[
            pltpu.VMEM((2,) + tokens.shape, BF16),
            pltpu.VMEM((4, 2 * QUARTER + ROOM, width), F32),
            pltpu.SemaphoreType.DMA((3,)),
        ],
        compiler_params=pltpu.CompilerParams(vmem_limit_bytes=8 << 20),
        cost_estimate=pl.CostEstimate(flops=0, bytes_accessed=1 << 20, transcendentals=0),
        name="pack",
    )(*(pltpu.with_memory_space_constraint(x, pltpu.HBM) for x in (tokens, grad, table)))


def bias_kernel(
    flag_ref, table_ref, weight_hbm, proj_hbm, low_ref, high_ref, weight_ref, proj_ref, pad_ref, sems
):
    copies = []
    for source, target, chunks in ((weight_hbm, weight_ref, 6), (proj_hbm, proj_ref, 2)):
        step = source.shape[1] // chunks
        for k in range(chunks):
            part = pl.ds(k * step, step)
            copies.append(
                pltpu.make_async_copy(source.at[:, part], target.at[:, part], sems.at[len(copies)])
            )
    for copy in copies:
        copy.start()
    heads, count = table_ref.shape
    width = pad_ref.shape[1]
    pad_ref[...] = jnp.zeros_like(pad_ref)
    pad_ref[:, :count] = table_ref[...]
    flat = pad_ref[...]
    shifts = WIN + EDGE
    moved = jnp.concatenate(
        [flat] + [pltpu.roll(flat, width - b, 1) for b in range(1, shifts)], axis=0
    )
    row = lax.broadcasted_iota(jnp.int32, (width, 2 * LANES), 0)
    col = lax.broadcasted_iota(jnp.int32, (width, 2 * LANES), 1)
    place = col + (SPAN - EDGE) * ((col * 10923) >> 16)
    pick = jnp.where((row == place) & (col < SPAN * EDGE), 1.0, 0.0).astype(BF16)
    first = moved.astype(BF16)
    rest = moved - first.astype(F32)
    second = rest.astype(BF16)
    third = (rest - second.astype(F32)).astype(BF16)
    packed = dot(first, pick, 1, 0) + (dot(second, pick, 1, 0) + dot(third, pick, 1, 0))
    half = WIN * EDGE
    lane = lax.broadcasted_iota(jnp.int32, (heads, LANES), 1)
    apart = jnp.where(flag_ref[0] > 0, -1e30, 0.0).astype(F32)
    for v in range(WIN):
        b = WIN - 1 - v
        side, inner = divmod(v, EDGE)
        near = packed[heads * b : heads * (b + 1)] + (apart if side == 1 else 0.0)
        far = packed[heads * (b + EDGE) : heads * (b + EDGE + 1)] + (apart if side == 0 else 0.0)
        for u in range(WIN):
            a = EDGE * (WIN - 1 - u)
            left = pltpu.roll(near, (2 * LANES - a) % (2 * LANES), 1) if a else near
            right = pltpu.roll(far, (half - a) % (2 * LANES), 1)
            start = heads * (side * half + u * EDGE + inner)
            low_ref[start : start + heads, :] = jnp.where(
                lane < half, left[:, :LANES], right[:, :LANES]
            )
            high_ref[start : start + heads, :] = right[:, LANES:]
    for copy in copies:
        copy.wait()


def relative_bias(flag, table, weight, proj):
    heads = table.shape[0]
    shape = jax.ShapeDtypeStruct((AREA * heads, LANES), F32)
    width = -(-table.shape[1] // LANES) * LANES
    hbm = pl.BlockSpec(memory_space=pltpu.HBM)
    vmem = pl.BlockSpec(memory_space=pltpu.VMEM)
    return pl.pallas_call(
        bias_kernel,
        out_shape=(
            shape,
            shape,
            jax.ShapeDtypeStruct(weight.shape, BF16),
            jax.ShapeDtypeStruct(proj.shape, BF16),
        ),
        in_specs=[pl.BlockSpec(memory_space=pltpu.SMEM), vmem, hbm, hbm],
        out_specs=(vmem,) * 4,
        scratch_shapes=[pltpu.VMEM((heads, width), F32), pltpu.SemaphoreType.DMA((8,))],
        compiler_params=pltpu.CompilerParams(vmem_limit_bytes=16 << 20),
        cost_estimate=pl.CostEstimate(
            flops=6 * 18 * heads * width * 256, bytes_accessed=6 << 20, transcendentals=0
        ),
        name="relative_bias",
    )(flag, table, *(pltpu.with_memory_space_constraint(x, pltpu.HBM) for x in (weight, proj)))


def window_kernel(
    blocks,
    order_ref,
    own_ref,
    diag_ref,
    lon_ref,
    lat_ref,
    gain_ref,
    weight_ref,
    proj_ref,
    low_ref,
    high_ref,
    qkv_ref,
    unit_ref,
    inverse_ref,
    grad_ref,
    *rest,
):
    weight_outs = rest[:-3]
    token_ref, turned_ref, placed_ref = rest[-3:]
    width = gain_ref.shape[1]
    heads = low_ref.shape[0] // AREA
    size = width // heads
    group = LANES // size
    factor = size ** (-0.5)
    for k, ref in enumerate((lon_ref, own_ref, diag_ref, lat_ref)):
        both = ref[...].astype(F32)
        token_ref[QUARTER * k : QUARTER * (k + 1), :] = both[:QUARTER]
        grad_ref[QUARTER * k : QUARTER * (k + 1), :] = both[QUARTER:]
    inputs = token_ref[:AREA, :]
    gain = gain_ref[...]
    centred = inputs - jnp.mean(inputs, axis=-1, keepdims=True)
    inverse = lax.rsqrt(jnp.mean(centred * centred, axis=-1, keepdims=True) + 1e-05)
    unit = centred * inverse
    unit_ref[...] = unit
    inverse_ref[...] = jnp.broadcast_to(inverse, inverse_ref.shape)
    normed = (unit * gain).astype(BF16)
    qkv_ref[...] = dot(normed, weight_ref[...], 1, 0).astype(BF16)
    upstream = dot(grad_ref[:AREA, :].astype(BF16), proj_ref[...], 1, 1).astype(BF16)
    lane = lax.broadcasted_iota(jnp.int32, (AREA, LANES), 1)
    zero = jnp.zeros((AREA, LANES), BF16)
    here = [(lane >= size * n) & (lane < size * (n + 1)) for n in range(group)]
    left = AREA - LANES
    packed = LANES // left
    span = packed * size
    row = lax.broadcasted_iota(jnp.int32, (LANES, span), 0)
    col = lax.broadcasted_iota(jnp.int32, (LANES, span), 1)
    own_block = row // left == col // size

    def diagonal(block):
        return jnp.where(own_block, jnp.concatenate([block] * packed, axis=0), jnp.zeros((LANES, span), BF16))

    def attend(scores, grad_probs, bias):
        scores = scores * factor + bias
        weights = jnp.exp(scores - jnp.max(scores, axis=0, keepdims=True))
        probs = weights * (1.0 / jnp.sum(weights, axis=0, keepdims=True))
        centre = jnp.sum(probs * grad_probs, axis=0, keepdims=True)
        return probs.astype(BF16), (probs * (grad_probs - centre) * factor).astype(BF16)

    for f in range(width // span):
        base = span * f
        query_all = qkv_ref[:, base : base + span]
        keys_all = qkv_ref[:, width + base : width + base + span]
        values_all = qkv_ref[:, 2 * width + base : 2 * width + base + span]
        up_all = upstream[:, base : base + span]
        keys_turned = keys_all.T
        query_left = diagonal(query_all[LANES:])
        up_left = diagonal(up_all[LANES:])
        bias = None
        for n in range(packed):
            part = high_ref[pl.ds(f * packed + n, AREA, stride=heads), :]
            if n == 0:
                bias = part
            else:
                bias = jnp.where(lane >= left * n, pltpu.roll(part, left * n, 1), bias)
        probs, grad_scores = attend(
            dot(keys_all, query_left, 1, 1), dot(values_all, up_left, 1, 1), bias
        )
        left_values = dot(probs, up_left, 1, 0)
        left_keys = dot(grad_scores, query_left, 1, 0)
        left_query = dot(keys_turned, grad_scores, 1, 0)
        for n in range(packed):
            part = left_query[size * n : size * (n + 1)]
            if n:
                part = pltpu.roll(part, LANES - left * n, 1)
            turned_ref[base + size * n : base + size * (n + 1), LANES:] = part[:, :left].astype(BF16)
        for g in range(span // LANES):
            inner = slice(LANES * g, LANES * (g + 1))
            start = base + LANES * g
            query = query_all[:LANES, inner]
            keys = keys_all[:, inner]
            values = values_all[:, inner]
            up = up_all[:LANES, inner]
            all_scores = dot(
                jnp.concatenate([jnp.where(m, keys, zero) for m in here], axis=0), query, 1, 1
            )
            all_grads = dot(
                jnp.concatenate([jnp.where(m, values, zero) for m in here], axis=0), up, 1, 1
            )
            low_probs, low_scores = [], []
            for n in range(group):
                first = start + size * n
                rows = slice(AREA * n, AREA * (n + 1))
                bias = low_ref[pl.ds(first // size, AREA, stride=heads), :]
                probs, grad_scores = attend(all_scores[rows], all_grads[rows], bias)
                low_probs.append(probs)
                low_scores.append(grad_scores)
                part = dot(keys_turned[LANES * g + size * n : LANES * g + size * (n + 1)], grad_scores, 1, 0)
                turned_ref[first : first + size, :LANES] = part.astype(BF16)
            all_values = dot(jnp.concatenate(low_probs, axis=0), up, 1, 0)
            all_keys = dot(jnp.concatenate(low_scores, axis=0), query, 1, 0)
            grad_values, grad_keys = all_values[:AREA], all_keys[:AREA]
            for n in range(1, group):
                rows = slice(AREA * n, AREA * (n + 1))
                grad_values = jnp.where(here[n], all_values[rows], grad_values)
                grad_keys = jnp.where(here[n], all_keys[rows], grad_keys)
            grad_values = (grad_values + left_values[:, inner]).astype(BF16)
            grad_keys = (grad_keys + left_keys[:, inner]).astype(BF16)
            qkv_ref[:, start : start + LANES] = turned_ref[start : start + LANES, :].T
            qkv_ref[:, width + start : width + start + LANES] = grad_keys
            qkv_ref[:, 2 * width + start : 2 * width + start + LANES] = grad_values
            turned_ref[width + start : width + start + LANES, :] = grad_keys.T
            turned_ref[2 * width + start : 2 * width + start + LANES, :] = grad_values.T
    if blocks is None:
        weight_outs[0][...] = dot(turned_ref[...], normed, 1, 0)
    else:
        send_ref, kept_ref, normed_ref = weight_outs
        rows = 3 * width // len(blocks)
        half = 3 * width // 2
        place = order_ref[0]
        odd = place % 2 == 1
        for slot, (even_offset, odd_offset) in enumerate(blocks):
            offset = jnp.where(odd, odd_offset, even_offset)
            start = pl.multiple_of((place ^ offset) * rows, rows)
            target, first = (kept_ref, slot * rows) if slot * rows < half else (placed_ref, slot * rows - half)
            target[first : first + rows, :] = turned_ref[pl.ds(start, rows), :]
        send_ref[...] = dot(placed_ref[...], normed, 1, 0).astype(BF16)
        normed_ref[...] = normed


def window_backward(order, quarters, gain, weight, proj, low, high, blocks):
    width = proj.shape[0]
    if blocks is None:
        weight_shapes = (jax.ShapeDtypeStruct((3 * width, width), F32),)
    else:
        weight_shapes = (
            jax.ShapeDtypeStruct((3 * width // 2, width), BF16),
            jax.ShapeDtypeStruct((3 * width // 2, AREA), BF16),
            jax.ShapeDtypeStruct((AREA, width), BF16),
        )
    vmem = pl.BlockSpec(memory_space=pltpu.VMEM)
    return pl.pallas_call(
        functools.partial(window_kernel, blocks),
        out_shape=(
            jax.ShapeDtypeStruct((AREA, 3 * width), BF16),
            jax.ShapeDtypeStruct((AREA, width), F32),
            jax.ShapeDtypeStruct((AREA, LANES), F32),
            jax.ShapeDtypeStruct((AREA + ROOM, width), F32),
        )
        + weight_shapes,
        in_specs=[pl.BlockSpec(memory_space=pltpu.SMEM)] + [vmem] * 9,
        out_specs=(vmem,) * (4 + len(weight_shapes)),
        scratch_shapes=[
            pltpu.VMEM((AREA + ROOM, width), F32),
            pltpu.VMEM((3 * width, AREA), BF16),
            pltpu.VMEM((3 * width // 2, AREA), BF16),
        ],
        compiler_params=pltpu.CompilerParams(vmem_limit_bytes=32 << 20),
        cost_estimate=pl.CostEstimate(
            flops=2 * AREA * width * width * 7, bytes_accessed=6 << 20, transcendentals=16 * AREA * AREA
        ),
        name="window_backward",
    )(order, *quarters, gain, weight, proj, low, high)


def norm_kernel(
    qkv_ref, weight_ref, gain_ref, unit_ref, inverse_ref, grad_ref, *rest
):
    if len(rest) > 4:
        kept_ref, normed_ref, *rest = rest
        keep_out = rest.pop(3)
        keep_out[...] = dot(kept_ref[...], normed_ref[...], 1, 0).astype(BF16)
    own_out, lon_out, side_out, token_ref = rest
    unit = unit_ref[...]
    scaled = dot(qkv_ref[...], weight_ref[...], 1, 1) * gain_ref[...]
    result = grad_ref[:AREA, :] + inverse_ref[:, :1] * (
        scaled
        - jnp.mean(scaled, axis=-1, keepdims=True)
        - unit * jnp.mean(scaled * unit, axis=-1, keepdims=True)
    )
    token_ref[:AREA, :] = result
    for k, ref in enumerate((lon_out, own_out, side_out.at[1], side_out.at[0])):
        ref[...] = token_ref[QUARTER * k : QUARTER * (k + 1), :].astype(BF16)


def norm_backward(qkv, weight, gain, unit, inverse, grad, kept):
    width = unit.shape[1]
    piece = jax.ShapeDtypeStruct((QUARTER, width), BF16)
    keep = (jax.ShapeDtypeStruct((3 * width // 2, width), BF16),) if kept else ()
    vmem = pl.BlockSpec(memory_space=pltpu.VMEM)
    return pl.pallas_call(
        norm_kernel,
        out_shape=(piece, piece, jax.ShapeDtypeStruct((2, QUARTER, width), BF16)) + keep,
        in_specs=[vmem] * (6 + len(kept)),
        out_specs=(vmem,) * (3 + len(keep)),
        scratch_shapes=[pltpu.VMEM((AREA + ROOM, width), F32)],
        compiler_params=pltpu.CompilerParams(vmem_limit_bytes=16 << 20),
        cost_estimate=pl.CostEstimate(
            flops=6 * AREA * width * width, bytes_accessed=3 << 20, transcendentals=0
        ),
        name="norm_backward",
    )(qkv, weight, gain, unit, inverse, grad, *kept)


def unpack_kernel(lon_ref, side_ref, own_ref, out_ref, line_ref):
    for u in range(WIN):
        left, right = (side_ref[0], own_ref[...]) if u < EDGE else (lon_ref[1], lon_ref[0])
        rows = slice(u % EDGE * EDGE, u % EDGE * EDGE + EDGE)
        line_ref[u, :EDGE, :] = left.astype(F32)[rows]
        line_ref[u, EDGE:WIN, :] = right.astype(F32)[rows]
    out_ref[...] = line_ref[:, :WIN, :].astype(BF16)


def unpack(lon, side, own):
    width = own.shape[1]
    vmem = pl.BlockSpec(memory_space=pltpu.VMEM)
    return pl.pallas_call(
        unpack_kernel,
        out_shape=jax.ShapeDtypeStruct((WIN, WIN, width), BF16),
        in_specs=[vmem] * 3,
        out_specs=vmem,
        scratch_shapes=[pltpu.VMEM((WIN, 2 * ROOM, width), F32)],
        compiler_params=pltpu.CompilerParams(vmem_limit_bytes=8 << 20),
        cost_estimate=pl.CostEstimate(flops=0, bytes_accessed=1 << 19, transcendentals=0),
        name="unpack",
    )(lon, side, own)


def exchange(block, even, odd, total):
    pairs = [(i, i ^ (odd if i % 2 else even)) for i in range(total)]
    return lax.ppermute(block, AXES, pairs)


def send_slots(slots, offsets, total):
    return [exchange(slots[k + 1], *offset, total) for k, offset in enumerate(offsets)]


def add_slots(own, arrived):
    summed = own.astype(F32)
    for piece in arrived:
        summed = summed + piece.astype(F32)
    return summed


def shards(tokens, norm_gain, qkv_weight, bias_table, proj_weight, out_grad):
    span_lon, span_lat, width = tokens.shape
    lons, lats = lax.axis_size("lon"), lax.axis_size("lat")
    total = lons * lats
    place = lax.axis_index("lon") * lats + lax.axis_index("lat")

    def route(step_lon, step_lat):
        return [
            (a * lats + b, (a + step_lon) % lons * lats + (b + step_lat) % lats)
            for a in range(lons)
            for b in range(lats)
        ]

    own, lon_start, lat_start, diag_start, table = pack(tokens, out_grad, bias_table)
    at_lon = lax.ppermute(lon_start, AXES, route(1, 0))
    at_diag = lax.ppermute(diag_start, AXES, route(1, -1))
    at_lat = lax.ppermute(lat_start, AXES, route(0, -1))
    quarters = [own, at_diag, at_lon, at_lat]
    flag = (lax.axis_index("lat") == lats - 1).astype(jnp.int32).reshape(1)
    low, high, weight, proj = relative_bias(flag, table, qkv_weight, proj_weight)
    rows = 3 * width // total
    staged = total % 32 == 0 and 3 * width % total == 0 and rows % 16 == 0
    if staged:
        far = total // 8
        blocks = tuple(
            (core + 2 * (k if core else PLANE[k]) + 8 * line, core + 2 * (PLANE[k] if core else k) + 8 * line)
            for core in range(2)
            for k in range(4)
            for line in line_order(far)
        )
    else:
        blocks = None
    gain = norm_gain.reshape(1, width)
    grad_qkv, unit, inverse, grad, *weight_grads = window_backward(
        place.astype(jnp.int32).reshape(1),
        quarters,
        gain,
        weight,
        proj,
        low,
        high,
        blocks,
    )
    own, to_lon, to_side, *keep = norm_backward(
        grad_qkv, weight, gain, unit, inverse, grad, weight_grads[1:]
    )
    factor = 1.0 / math.sqrt(span_lon * lons * span_lat * lats)
    if staged:
        send, keep = weight_grads[0], keep[0]
        shape = (4, far, rows, width)
        pair = add_slots(keep.reshape(shape), [exchange(send.reshape(shape), 1, 1, total)]).astype(BF16)
        planes = [(2 * PLANE[k], 2 * k) for k in range(1, 4)]
        plane = add_slots(pair[0], send_slots(pair, planes, total)).astype(BF16)
        arrived = send_slots(plane, [(8 * k, 8 * k) for k in line_order(far)[1:]], total)
        summed = add_slots(plane[0], arrived).reshape(-1)
    else:
        summed = lax.psum_scatter(
            weight_grads[0].reshape(-1), AXES, scatter_dimension=0, tiled=True
        )
    from_side = lax.ppermute(to_side, AXES, route(0, 1))
    from_lon = lax.ppermute(jnp.stack([to_lon, from_side[1]]), AXES, route(-1, 0))
    token_grad = unpack(from_lon, from_side, own)
    return (token_grad, summed * factor)


def solution(mesh):
    placed = (P("lon", "lat", None), P(), P(), P(), P(), P("lon", "lat", None))
    return jax.shard_map(
        shards,
        mesh=mesh,
        in_specs=placed,
        out_specs=(P("lon", "lat", None), P(("lon", "lat"))),
        check_vma=False,
    )
```
